512 devices in a mesh: node: 16 (over y, core), tile: 32 (over z, x).
Axes of the slice: x: 4, y: 8, z: 8, core: 2. Of those that a mesh axis runs over, the one named last changes fastest.
Arguments:
- child_cost: float32 [128, 1024, 1024], P('node', 'tile'), as said below
- child_weight: int32 [128], P('node'), may hold values from 1 to 16
- parent_of: int32 [128], P('node'), may hold values from 0 to 31, as said below
- dyn_a: bfloat16 [1024, 1024], replicated, may hold values from -0.1875 to 0.1875
- dyn_b: bfloat16 [1024, 256], replicated, may hold values from -0.1875 to 0.1875
- state_weight: float32 [32, 1024], P('node', 'tile'), may hold values from 0.2 to 5
- input_weight: float32 [32, 256], P('node'), may hold values from 0.3 to 3
- parent_cov: bfloat16 [32, 1024, 1024], P('node', 'tile'), as said below
- noise_cov: float32 [128, 1024], P('node', 'tile'), may hold values from 0.05 to 1
Outputs:
- parent_cost: float32 [32, 1024, 1024], P('node', 'tile')
- parent_gain: float32 [32, 256, 1024], P('node', 'tile')
- child_cov: float32 [128, 1024, 1024], P('node', 'tile')
The draws below stay inside these ranges and needn't reach their ends.
Inputs may be any that keep to these rules, and one draw needn't show every extreme that they name: `parent_of`: the 128 children are listed by parent: the numbers never fall; every parent has 2 to 8 children, some parent exactly 8 and some exactly 2; parents 4k to 4k + 3 together have exactly 16 children. `child_cost`: each matrix is symmetric positive definite. `parent_cov`: each matrix is symmetric positive definite.
All inputs are finite; a program needn't handle non-finite values.
Results may differ from the reference program's by a relative error of at most 0.0022.
Values may be sent and summed in bfloat16 or wider, within the bound.
A program may use at most 64 MiB of HBM per device.

```python
import math
import jax
import jax.numpy as jnp
import numpy as np
from jax import lax

N = 1024
M = 256
PARENTS = 32
CHILDREN = 128


def definite_block(key, count, factor_scale):
    keys = jax.random.split(key, 2)
    factor = jax.random.normal(keys[0], (count, N, N), jnp.float32)
    gram = jnp.einsum('cik,cjk->cij', factor, factor, precision=lax.Precision.HIGHEST) / N
    diag_values = jnp.exp(jax.random.uniform(keys[1], (count, N), jnp.float32, math.log(0.5), math.log(4.0)))
    block = gram + diag_values[:, :, None] * jnp.eye(N, dtype=jnp.float32)[None]
    return factor_scale * block


def draw_child_cost(key, part):
    return definite_block(jax.random.fold_in(key, 5), CHILDREN, 1.0)


def draw_parent_cov(key, part):
    return definite_block(jax.random.fold_in(key, 7), PARENTS, 0.5).astype(jnp.bfloat16)


def draw_parent_of(key, part):
    table = jnp.array(np.array([[8, 2, 3, 3], [4, 4, 4, 4], [5, 3, 6, 2], [2, 2, 6, 6], [7, 3, 2, 4], [3, 5, 5, 3]], np.int32))
    key_one, key_two = jax.random.split(jax.random.fold_in(key, 9))
    block_count = PARENTS // 4
    picked = jax.random.randint(key_one, (block_count,), 0, 6, jnp.int32)
    picked = jnp.where(jnp.arange(block_count, dtype=jnp.int32) == 0, 0, picked)
    patterns = table[picked]
    scores = jax.random.randint(key_two, (block_count, 4), 0, 1 << 20, jnp.int32) * 4 + jnp.arange(4, dtype=jnp.int32)[None, :]
    ranking = jnp.argsort(scores, axis=1)
    counts = jnp.take_along_axis(patterns, ranking, axis=1).reshape(PARENTS)
    ends = jnp.cumsum(counts).astype(jnp.int32)
    child_ids = jnp.arange(CHILDREN, dtype=jnp.int32)
    return jnp.sum((ends[None, :] <= child_ids[:, None]).astype(jnp.int32), axis=1).astype(jnp.int32)


def touch_ends(values, own_key, least, high):
    extent = values.shape
    index_at = [jax.random.randint(jax.random.fold_in(own_key, axis), (), 0, extent[axis]) for axis in range(len(extent))]
    values = values.at[tuple(index_at)].set(least)
    longest = extent.index(max(extent))
    index_at[longest] = (index_at[longest] + 1) % extent[longest]
    return values.at[tuple(index_at)].set(high)


def steps_of(own_key, extent, shards, least, top_value):
    level, own = 1.0, jax.random.fold_in(own_key, 6)
    for dim, parts in shards:
        draws = jnp.exp(jax.random.uniform(jax.random.fold_in(own, dim), (parts,), jnp.float32, least / len(shards), top_value / len(shards)))
        level = level * jnp.repeat(draws, extent[dim] // parts).reshape([-1 if axis == dim else 1 for axis in range(len(extent))])
    return level


def gaussian(stream_key, dims, width, reach, held_as=jnp.bfloat16):
    return jnp.clip(width * jax.random.normal(stream_key, dims, jnp.float32), -reach, reach).astype(held_as)


def setup_inputs(seed: int = 0) -> dict:
    arg_keys = jax.random.split(jax.random.key(seed), 10)
    child_cost = draw_child_cost(jax.random.fold_in(arg_keys[9], 71), 0)
    child_weight = touch_ends(jax.random.randint(arg_keys[1], (CHILDREN,), 1, 17), jax.random.fold_in(arg_keys[1], 1), 1, 16).astype(jnp.int32)
    parent_of = draw_parent_of(jax.random.fold_in(arg_keys[9], 71), 0)
    dyn_a = gaussian(arg_keys[3], (N, N), N ** -0.5, 0.1875)
    dyn_b = gaussian(arg_keys[4], (N, M), N ** -0.5, 0.1875)
    state_weight = jnp.clip(jnp.exp(math.log(5.0) - 3.218876 * jax.random.uniform(arg_keys[5], (PARENTS, N), jnp.float32) ** steps_of(arg_keys[5], (PARENTS, N), ((0, 16), (1, 32)), -0.2, 0.2)), 0.2, 5.0)
    input_weight = jnp.clip(jnp.exp(math.log(3.0) - 2.3025851 * jax.random.uniform(arg_keys[6], (PARENTS, M), jnp.float32) ** steps_of(arg_keys[6], (PARENTS, M), ((0, 16),), -0.2, 0.2)), 0.3, 3.0)
    parent_cov = draw_parent_cov(jax.random.fold_in(arg_keys[9], 71), 0)
    noise_cov = jnp.clip(jnp.exp(math.log(1.0) - 2.9957323 * jax.random.uniform(arg_keys[8], (CHILDREN, N), jnp.float32) ** steps_of(arg_keys[8], (CHILDREN, N), ((0, 16), (1, 32)), -0.2, 0.2)), 0.05, 1.0)
    return dict(child_cost=child_cost, child_weight=child_weight, parent_of=parent_of, dyn_a=dyn_a, dyn_b=dyn_b, state_weight=state_weight, input_weight=input_weight, parent_cov=parent_cov, noise_cov=noise_cov)


def reference(child_cost, child_weight, parent_of, dyn_a, dyn_b, state_weight, input_weight, parent_cov, noise_cov):
    highest = lax.Precision.HIGHEST
    labels = jnp.arange(PARENTS, dtype=jnp.int32)
    picks = (parent_of[:, None] == labels[None, :]).astype(jnp.float32) * child_weight.astype(jnp.float32)[:, None]
    weight_sum = jnp.sum(picks, axis=0)
    expected = jnp.einsum('cq,cij->qij', picks, child_cost, precision=highest) / weight_sum[:, None, None]
    a_full = dyn_a.astype(jnp.float32)
    b_full = dyn_b.astype(jnp.float32)
    b_side = jnp.einsum('km,qkn->qmn', b_full, expected, precision=highest)
    curvature = jnp.einsum('qmn,nl->qml', b_side, b_full, precision=highest)
    curvature = curvature + input_weight[:, :, None] * jnp.eye(M, dtype=jnp.float32)[None]
    coupling = jnp.einsum('qmn,nj->qmj', b_side, a_full, precision=highest)
    factor = jnp.linalg.cholesky(curvature)
    halfway = lax.linalg.triangular_solve(factor, coupling, left_side=True, lower=True)
    gain = lax.linalg.triangular_solve(factor, halfway, left_side=True, lower=True, transpose_a=True)
    cost_a = jnp.einsum('qkn,nj->qkj', expected, a_full, precision=highest)
    quadratic = jnp.einsum('ki,qkj->qij', a_full, cost_a, precision=highest)
    correction = jnp.einsum('qmi,qmj->qij', coupling, gain, precision=highest)
    parent_cost = quadratic - correction + state_weight[:, :, None] * jnp.eye(N, dtype=jnp.float32)[None]
    closed = (a_full[None] - jnp.einsum('im,qmj->qij', b_full, gain, precision=highest)).astype(jnp.bfloat16)
    moment = jnp.einsum('qik,qkj->qij', closed.astype(jnp.float32), parent_cov.astype(jnp.float32), precision=highest)
    inner = jnp.einsum('qin,qmn->qim', moment, gain, precision=highest)
    spread = jnp.einsum('qin,jn->qij', moment, a_full, precision=highest) - jnp.einsum('qim,jm->qij', inner, b_full, precision=highest)
    child_cov = spread[parent_of] + noise_cov[:, :, None] * jnp.eye(N, dtype=jnp.float32)[None]
    return (parent_cost, gain, child_cov)
```

```python
import functools

import jax
import jax.numpy as jnp
from jax import lax
from jax.experimental import pallas as pl
from jax.experimental.pallas import tpu as pltpu
from jax.sharding import PartitionSpec as P

F32, BF16 = jnp.float32, jnp.bfloat16
MESH = pl.DeviceIdType.MESH


def split(v):
    high = v.astype(BF16)
    return high, (v - high.astype(F32)).astype(BF16)


def mm(a, b, dims=((1,), (0,))):
    return lax.dot_general(a, b, (dims, ((), ())), preferred_element_type=F32)


def mm2(a, b, dims=((1,), (0,))):
    return mm(a[0], b, dims) + mm(a[1], b, dims)


def mm3(a, b, dims=((1,), (0,))):
    return mm(a[0], b[0], dims) + (mm(a[0], b[1], dims) + mm(a[1], b[0], dims))


def total(terms):
    while len(terms) > 1:
        terms = [
            terms[i] + terms[i + 1] if i + 1 < len(terms) else terms[i]
            for i in range(0, len(terms), 2)
        ]
    return terms[0]


def small_inverse(d):
    b = len(d)
    if b == 2:
        r = 1.0 / (d[0][0] * d[1][1] - d[0][1] * d[0][1])
        off = -d[0][1] * r
        return [[d[1][1] * r, off], [off, d[0][0] * r]]
    h = b // 2
    span = range(h)
    x = small_inverse([[d[i][j] for j in span] for i in span])
    y = [[d[i][h + j] for j in span] for i in span]
    w = [[total([x[i][k] * y[k][j] for k in span]) for j in span] for i in span]
    s = [[None] * h for _ in span]
    for i in span:
        for j in range(i, h):
            s[i][j] = s[j][i] = d[h + i][h + j] - total([y[k][i] * w[k][j] for k in span])
    q = small_inverse(s)
    wq = [[total([w[i][k] * q[k][j] for k in span]) for j in span] for i in span]
    out = [[None] * b for _ in range(b)]
    for i in span:
        for j in range(i, h):
            out[i][j] = out[j][i] = x[i][j] + total([wq[i][k] * w[j][k] for k in span])
        for j in span:
            out[i][h + j] = out[h + j][i] = -wq[i][j]
            out[h + i][h + j] = q[i][j]
    return out


def sweep(a, trips, b=4, unroll=8):
    n = a.shape[0]
    lane = lax.broadcasted_iota(jnp.int32, (1, n), 1)
    lanes = lax.broadcasted_iota(jnp.int32, (n, n), 1)
    sub = lax.broadcasted_iota(jnp.int32, (n, 1), 0)

    def body(_, a):
        for low in range(0, unroll, b):
            ks = range(low, low + b)
            d = [[jnp.broadcast_to(a[i : i + 1, j : j + 1], (1, n)) for j in ks] for i in ks]
            inv = small_inverse(d)
            rows = [a[j : j + 1, :] for j in ks]
            in_rows = (sub >= low) & (sub < low + b)
            cols = [jnp.where(sub == k, -1.0, jnp.where(in_rows, 0.0, a[:, k : k + 1])) for k in ks]
            new = []
            for i in range(b):
                t = total([inv[i][j] * rows[j] for j in range(b)])
                for j in range(b):
                    t = jnp.where(lane == low + j, inv[i][j], t)
                new.append(t)
            a = jnp.where(((lanes >= low) & (lanes < low + b)) | in_rows, 0.0, a)
            for i in range(b):
                a = a - cols[i] * new[i]
        a = jnp.concatenate([a[unroll:], a[:unroll]], axis=0)
        return pltpu.roll(a, n - unroll, 1)

    return lax.fori_loop(0, trips, body, a)


HOPS = ((4, 3), (3, 4))


def kernel(
    cc, cw, po, a_in, b_in, sw, iw, pcov, nz,
    pc_out, pg_out, ch_out,
    ccv, a5, b5, at5, lt, e5, p5, acc, mine, theirs, wt, wr, iwr, eb,
    bh, bl, cpl, gv, gh, gl, pcv, pcr, pgr, spv, spr, chv,
    load_sem, loc_sem, out_sem, sa_s, sa_r, sb_s, sb_r, pa_s, pa_r,
    er_s, er_r, ef_s, ef_r, pr_s, pr_r, pf_s, pf_r,
    gs_s, gs_r, cs_s, cs_r, ss_s, ss_r, sf_s, sf_r,
):
    n, t = lax.axis_index("node"), lax.axis_index("tile")
    c, y = lax.rem(n, 2), n // 2
    z, x = t // 4, lax.rem(t, 4)
    oc = 1 - c
    own, jq = x // 2, lax.rem(x, 2)

    def dev(core, zz, xx):
        return (2 * y + core, 4 * zz + xx)

    def xs(dx):
        return lax.rem(x + dx + 4, 4)

    def zs(dz):
        return lax.rem(z + dz + 8, 8)

    def remote(src, dst, ssem, rsem, where):
        return pltpu.make_async_remote_copy(
            src_ref=src, dst_ref=dst, send_sem=ssem, recv_sem=rsem,
            device_id=where, device_id_type=MESH,
        )

    zlane = pl.multiple_of(z * 128, 128)

    barrier = pltpu.get_barrier_semaphore()
    for dx in range(4):
        for core in ((oc,) if dx == 0 else (c, oc)):
            pl.semaphore_signal(barrier, inc=1, device_id=dev(core, z, xs(dx)), device_id_type=MESH)
    for dz in (1, -1):
        pl.semaphore_signal(barrier, inc=1, device_id=dev(c, zs(dz), x), device_id_type=MESH)

    loads = [
        pltpu.make_async_copy(cc, ccv, load_sem.at[0]),
        pltpu.make_async_copy(b_in, b5, load_sem.at[1]),
        pltpu.make_async_copy(a_in, a5, load_sem.at[2]),
    ]
    for cp in loads:
        cp.start()

    first = 4 * y
    coef = [
        [jnp.where(po[k] == first + q, cw[k].astype(F32), 0.0) for q in range(4)]
        for k in range(8)
    ]
    sub8 = lax.broadcasted_iota(jnp.int32, (8, 128), 0)
    tile = jnp.zeros((8, 128), F32)
    for q in range(4):
        s = total([coef[k][q] for k in range(8)])
        tile = jnp.where(sub8 == q, s, tile)
    wt[...] = tile

    loads[0].wait()

    def weigh(i, _):
        cols = pl.ds(pl.multiple_of(i * 256, 256), 256)
        for h in range(2):
            sums = [None] * 4
            for k in range(8):
                v = ccv[k, 16 * h : 16 * h + 16, cols]
                for q in range(4):
                    term = coef[k][q] * v
                    sums[q] = term if k == 0 else sums[q] + term
            for q in range(4):
                mine[q, h, :, cols] = sums[q]
        return 0

    lax.fori_loop(0, 4, weigh, 0)

    pl.semaphore_wait(barrier, 9)

    pair = dev(oc, z, x)
    swap = [
        remote(mine.at[:, oc], theirs, sa_s.at[0], sa_r.at[0], pair),
        remote(wt, wr, sa_s.at[1], sa_r.at[1], pair),
        remote(iw, iwr, sa_s.at[2], sa_r.at[2], pair),
    ]
    for cp in swap:
        cp.start()

    def cov_copy(dx, other):
        q = xs(dx)
        core = oc if other else c
        return remote(
            pcov.at[lax.rem(q, 2), pl.ds(pl.multiple_of(16 * core, 16), 16)],
            p5.at[z, x, core], pa_s.at[dx, int(other)], pa_r.at[dx], dev(core, z, q),
        )

    def cov_local():
        return pltpu.make_async_copy(
            pcov.at[jq, pl.ds(pl.multiple_of(16 * c, 16), 16)], p5.at[z, x, c], loc_sem.at[0]
        )

    for dx in (2, 1, 3, 0):
        @pl.when(xs(dx) // 2 == c)
        def _(dx=dx):
            cov_copy(dx, True).start()
            (cov_copy(dx, False) if dx else cov_local()).start()

    loads[1].wait()
    lt[0:256, :] = b5[...].reshape(1024, 256).T
    loads[2].wait()

    def turn(i, _):
        block = a5[pl.ds(i, 1)].reshape(128, 1024)
        at5[:, :, :, :, pl.ds(pl.multiple_of(i * 128, 128), 128)] = block.T.reshape(8, 4, 2, 16, 128)
        return 0

    lax.fori_loop(0, 8, turn, 0)
    lt[256:320, :] = at5[z, :, c].reshape(64, 1024)

    for cp in swap:
        cp.wait_recv()
    wsum = wt[...] + wr[...]
    for q in range(4):
        e = (mine[q, c] + theirs[q]) / wsum[q : q + 1, 0:1]
        high = e.astype(BF16)
        eb[q, :, 0:1024] = high
        mine[q, c] = e - high.astype(F32)
    for q in range(4):
        eb[q, :, 1024:1152] = mine[q, c, :, pl.ds(zlane, 128)].astype(BF16)

    spread_e = [
        remote(eb.at[xs(dx)], e5.at[z, x, c], sb_s.at[dx], sb_r.at[dx], dev(c, z, xs(dx)))
        for dx in (2, 1, 3)
    ]
    for cp in spread_e:
        cp.start()
    e5[z, x, c] = eb[x]
    for dx in (2, 1, 3):
        remote(eb.at[xs(dx)], e5.at[z, xs(-dx), c], sb_s.at[dx], sb_r.at[dx], dev(c, z, xs(dx))).wait_recv()

    def ring_copy(buf, ssem, rsem, d, s, h):
        sign = 1 - 2 * d
        part = buf.at[zs(-sign * (s - 1)), pl.ds(2 * h, 2), c]
        return remote(part, part, ssem.at[d, s - 1, h], rsem.at[d, s - 1, h], dev(c, zs(sign), x))

    def ring_got(buf, ssem, rsem, d, s, h):
        sign = 1 - 2 * d
        part = buf.at[zs(-sign * s), pl.ds(2 * h, 2), c]
        return remote(part, part, ssem.at[d, s - 1, h], rsem.at[d, s - 1, h], dev(c, zs(sign), x))

    def hand(buf, ssem, rsem, d, s, h, core):
        sign = 1 - 2 * d
        part = buf.at[zs(-sign * s), pl.ds(2 * h, 2), core]
        return remote(part, part, ssem.at[d, s, h], rsem.at[d, s, h], pair)

    def ring_start(buf, ssem, rsem, fs, fr):
        for h in range(2):
            for d in ((0, 1) if h == 0 else (1, 0)):
                ring_copy(buf, ssem, rsem, d, 1, h).start()
        for h in range(2):
            hand(buf, fs, fr, 0, 0, h, c).start()

    def ring_step(buf, ssem, rsem, fs, fr, s):
        for h in range(2):
            for d in ((0, 1) if h == 0 else (1, 0)):
                if s <= HOPS[d][h]:
                    ring_got(buf, ssem, rsem, d, s, h).wait_recv()
                    if s < HOPS[d][h]:
                        ring_copy(buf, ssem, rsem, d, s + 1, h).start()
                    hand(buf, fs, fr, d, s, h, c).start()

    def hand_wait(buf, fs, fr, s):
        for h in range(2):
            if s == 0:
                hand(buf, fs, fr, 0, 0, h, oc).wait_recv()
            else:
                for d in range(2):
                    if s <= HOPS[d][h]:
                        hand(buf, fs, fr, d, s, h, oc).wait_recv()

    def drain(buf, ssem, rsem, fs, fr):
        for h in range(2):
            hand(buf, fs, fr, 0, 0, h, c).wait_send()
            for d in range(2):
                for s in range(1, HOPS[d][h] + 1):
                    ring_copy(buf, ssem, rsem, d, s, h).wait_send()
                    hand(buf, fs, fr, d, s, h, c).wait_send()

    e_ring = (e5, er_s, er_r, ef_s, ef_r)
    p_ring = (p5, pr_s, pr_r, pf_s, pf_r)

    def gather_add(zc, begin):
        k = pl.ds(pl.multiple_of(zc * 128, 128), 128)
        left = lt[:, k]

        def part(i, _):
            cols = pl.ds(pl.multiple_of(i * 256, 256), 256)
            v = mm(left, e5[zc, :, :, :, cols].reshape(128, 256))
            acc[:, cols] = v if begin else acc[:, cols] + v
            return 0

        lax.fori_loop(0, 4, part, 0)
        acc[:, k] += mm(left, e5[zc, :, :, :, 1024:1152].reshape(128, 128))

    ring_start(*e_ring)
    hand_wait(e5, ef_s, ef_r, 0)
    gather_add(z, True)
    for s in range(1, 5):
        ring_step(*e_ring, s)
        if s == 4:
            for dx in (2, 1, 3):
                remote(pcov.at[0, 0:16], p5.at[z, xs(-dx), c], pa_s.at[dx, 0], pa_r.at[dx], pair).wait_recv()

            @pl.when(own == c)
            def _():
                cov_local().wait()

            @pl.when(own != c)
            def _():
                remote(pcov.at[0, 0:16], p5.at[z, x, c], pa_s.at[0, 0], pa_r.at[0], pair).wait_recv()

            ring_start(*p_ring)
        hand_wait(e5, ef_s, ef_r, s)
        if s < 4:
            gather_add(zs(-s), False)
            gather_add(zs(s), False)
        else:
            gather_add(zs(4), False)

    hi, lo = split(acc[...])
    bh[...] = hi
    bl[...] = lo
    bfull = b5[...].reshape(1024, 256)
    small = mm(bh[...], bfull) + mm(bl[...], bfull)
    weights = jnp.where(own == c, iw[pl.ds(jq, 1), :], iwr[pl.ds(jq, 1), :])
    r256 = lax.broadcasted_iota(jnp.int32, (256, 256), 0)
    c256 = lax.broadcasted_iota(jnp.int32, (256, 256), 1)
    curv = small[0:256] + jnp.where(r256 == c256, weights, 0.0)
    cpl_own = split(small[256:320])

    def times_a(i, _):
        cols = pl.ds(pl.multiple_of(i * 256, 256), 256)
        right = a5[:, :, :, :, cols].reshape(1024, 256)
        cpl[:, cols] = mm(bh[...], right) + mm(bl[...], right)
        return 0

    lax.fori_loop(0, 4, times_a, 0)

    ring_step(*p_ring, 1)
    s11, s12, s22 = curv[:128, :128], curv[:128, 128:], curv[128:, 128:]
    inv = sweep(s11, 8)
    ring_step(*p_ring, 2)
    inv = sweep(inv, 8)
    ring_step(*p_ring, 3)
    inv_s, s12_s = split(inv), split(s12)
    w_s = split(mm3(inv_s, s12_s))
    inv2 = sweep(s22 - mm3(s12_s, w_s, ((0,), (0,))), 8)
    ring_step(*p_ring, 4)
    inv2_s = split(sweep(inv2, 8))

    def back(i, _):
        cols = pl.ds(pl.multiple_of(i * 256, 256), 256)
        top = split(cpl[0:128, cols])
        low = cpl[128:256, cols] - mm3(w_s, top, ((0,), (0,)))
        g2 = mm3(inv2_s, split(low))
        g1 = mm3(inv_s, top) - mm3(w_s, split(g2))
        gv[0:128, cols] = g1
        gv[128:256, cols] = g2
        for half, g in ((0, g1), (128, g2)):
            high, rest = split(g)
            gh[half : half + 128, cols] = high
            gl[half : half + 128, cols] = rest
        return 0

    lax.fori_loop(0, 4, back, 0)

    def gain_copy(dx):
        xx = xs(dx)
        rows = pl.ds(pl.multiple_of(32 * z + 8 * xx, 8), 8)
        return remote(gv.at[rows], pgr.at[jq], gs_s.at[dx], gs_r.at[dx], dev(c, z, xx))

    @pl.when(own == c)
    def _():
        for dx in (2, 1, 3):
            gain_copy(dx).start()
        pgr[jq] = gv[pl.ds(pl.multiple_of(32 * z + 8 * x, 8), 8), :]

    def cost(i, _):
        cols = pl.ds(pl.multiple_of(i * 256, 256), 256)
        v = cpl[256:320, cols] - mm3(cpl_own, (gh[:, cols], gl[:, cols]))
        pcv[:, :, cols] = v.reshape(4, 16, 256)
        return 0

    lax.fori_loop(0, 4, cost, 0)

    def cost_copy(dx):
        return remote(pcv.at[xs(dx)], pcr.at[jq, c], cs_s.at[dx], cs_r.at[dx, c], dev(own, z, xs(dx)))

    for dx in (2, 1, 3):
        cost_copy(dx).start()

    @pl.when(own == c)
    def _():
        pcr[jq, c] = pcv[x]

    @pl.when(own != c)
    def _():
        cost_copy(0).start()

    a_rows = a5[z, :, c].reshape(64, 1024).astype(F32)
    b_rows = b5[z, :, c].reshape(64, 256)
    closed = (a_rows - (mm(b_rows, gh[...]) + mm(b_rows, gl[...]))).astype(BF16)
    for s in range(5):
        hand_wait(p5, pf_s, pf_r, s)
    moment_s = split(mm(closed, p5[...].reshape(1024, 1024)))
    nt = ((1,), (1,))
    inner_s = split(mm3(moment_s, (gh[...], gl[...]), nt))

    def out_cols(i, _):
        cols = pl.ds(pl.multiple_of(i * 256, 256), 256)
        v = mm2(moment_s, at5[:, :, :, :, cols].reshape(1024, 256)) - mm2(inner_s, lt[0:256, cols])
        spv[:, :, cols] = v.reshape(4, 16, 256)
        return 0

    lax.fori_loop(0, 4, out_cols, 0)

    def spread_copy(dx):
        return remote(spv.at[xs(dx)], spr.at[x, c], ss_s.at[dx], ss_r.at[dx], dev(c, z, xs(dx)))

    def spread_got(dx):
        return remote(spv.at[xs(dx)], spr.at[xs(-dx), c], ss_s.at[dx], ss_r.at[dx], dev(c, z, xs(dx)))

    def spread_hand(dx, core):
        return remote(spr.at[xs(-dx), core], spr.at[xs(-dx), core], sf_s.at[dx], sf_r.at[dx], pair)

    for dx in (2, 1, 3):
        spread_copy(dx).start()
    spr[x, c] = spv[x]
    spread_hand(0, c).start()

    for dx in (1, 2, 3):
        @pl.when(xs(-dx) // 2 == c)
        def _(dx=dx):
            remote(gv.at[0:8], pgr.at[lax.rem(xs(-dx), 2)], gs_s.at[dx], gs_r.at[dx], pair).wait_recv()
            for core in range(2):
                remote(pcv.at[0], pcr.at[lax.rem(xs(-dx), 2), core], cs_s.at[dx], cs_r.at[dx, core], pair).wait_recv()

    @pl.when(own == c)
    def _():
        remote(pcv.at[0], pcr.at[jq, oc], cs_s.at[0], cs_r.at[0, oc], pair).wait_recv()

    out_pg = pltpu.make_async_copy(pgr, pg_out, out_sem.at[8])
    out_pg.start()
    diag = lax.broadcasted_iota(jnp.int32, (32, 128), 1) == (
        32 * x + lax.broadcasted_iota(jnp.int32, (32, 128), 0)
    )
    pick = lax.broadcasted_iota(jnp.int32, (32, 32), 1) == lax.broadcasted_iota(jnp.int32, (32, 32), 0)

    def on_diag(row):
        column = jnp.sum(jnp.where(pick, row, 0.0), axis=1, keepdims=True)
        return jnp.where(diag, column, 0.0)

    for j in range(2):
        pcr[j, :, :, pl.ds(zlane, 128)] += on_diag(sw[j : j + 1, :]).reshape(2, 16, 128)
    out_pc = pltpu.make_async_copy(pcr, pc_out, out_sem.at[9])
    out_pc.start()

    for dx in (1, 3, 2):
        spread_got(dx).wait_recv()
        spread_hand(dx, c).start()
    for dx in range(4):
        spread_hand(dx, oc).wait_recv()

    pos = [[po[k] == first + q for q in range(4)] for k in range(8)]
    outs = []
    for k in range(8):
        def fill(i, _, k=k):
            cols = pl.ds(pl.multiple_of(i * 256, 256), 256)
            v = spr[0, :, :, cols]
            for q in range(1, 4):
                v = jnp.where(pos[k][q], spr[q, :, :, cols], v)
            chv[k, :, :, cols] = v
            return 0

        lax.fori_loop(0, 4, fill, 0)
        chv[k, :, :, pl.ds(zlane, 128)] += on_diag(nz[k : k + 1, :]).reshape(2, 16, 128)
        cp = pltpu.make_async_copy(chv.at[k], ch_out.at[k], out_sem.at[k])
        cp.start()
        outs.append(cp)

    for cp in swap + spread_e:
        cp.wait_send()
    for dx in range(4):
        @pl.when(xs(dx) // 2 == c)
        def _(dx=dx):
            cov_copy(dx, True).wait_send()
            if dx:
                cov_copy(dx, False).wait_send()
    drain(*e_ring)
    drain(*p_ring)

    @pl.when(own == c)
    def _():
        for dx in (2, 1, 3):
            gain_copy(dx).wait_send()

    @pl.when(own != c)
    def _():
        cost_copy(0).wait_send()

    for dx in (2, 1, 3):
        cost_copy(dx).wait_send()
        spread_copy(dx).wait_send()
    for dx in range(4):
        spread_hand(dx, c).wait_send()
    out_pg.wait()
    out_pc.wait()
    for cp in outs:
        cp.wait()


def on_device(cc, cw, po, a, b, sw, iw, pcov, nz):
    any_, vmem, smem = (pl.BlockSpec(memory_space=m) for m in (pl.ANY, pltpu.VMEM, pltpu.SMEM))
    v, dma = pltpu.VMEM, pltpu.SemaphoreType.DMA
    scratch = [
        v((8, 32, 1024), F32),
        v((8, 4, 2, 16, 1024), BF16),
        v((8, 4, 2, 16, 256), BF16),
        v((8, 4, 2, 16, 1024), BF16),
        v((320, 1024), BF16),
        v((8, 4, 2, 16, 1152), BF16),
        v((8, 4, 2, 16, 1024), BF16),
        v((320, 1024), F32),
        v((4, 2, 16, 1024), F32),
        v((4, 16, 1024), F32),
        v((8, 128), F32),
        v((8, 128), F32),
        v((2, 256), F32),
        v((4, 16, 1152), BF16),
        v((320, 1024), BF16),
        v((320, 1024), BF16),
        v((320, 1024), F32),
        v((256, 1024), F32),
        v((256, 1024), BF16),
        v((256, 1024), BF16),
        v((4, 16, 1024), F32),
        v((2, 2, 16, 1024), F32),
        v((2, 8, 1024), F32),
        v((4, 16, 1024), F32),
        v((4, 2, 16, 1024), F32),
        v((8, 2, 16, 1024), F32),
        dma((3,)), dma((1,)), dma((10,)),
        dma((3,)), dma((3,)),
        dma((4,)), dma((4,)),
        dma((4, 2)), dma((4,)),
        dma((2, 4, 2)), dma((2, 4, 2)), dma((2, 5, 2)), dma((2, 5, 2)),
        dma((2, 4, 2)), dma((2, 4, 2)), dma((2, 5, 2)), dma((2, 5, 2)),
        dma((4,)), dma((4,)),
        dma((4,)), dma((4, 2)),
        dma((4,)), dma((4,)), dma((4,)), dma((4,)),
    ]
    pc, pg, ch = pl.pallas_call(
        kernel,
        out_shape=(
            jax.ShapeDtypeStruct((2, 2, 16, 1024), F32),
            jax.ShapeDtypeStruct((2, 8, 1024), F32),
            jax.ShapeDtypeStruct((8, 2, 16, 1024), F32),
        ),
        in_specs=[any_, smem, smem, any_, any_, vmem, vmem, vmem, vmem],
        out_specs=(any_, any_, any_),
        scratch_shapes=scratch,
        compiler_params=pltpu.CompilerParams(collective_id=0, has_side_effects=True),
    )(
        cc, cw, po, a.reshape(8, 4, 2, 16, 1024), b.reshape(8, 4, 2, 16, 256), sw, iw, pcov, nz
    )
    return pc.reshape(2, 32, 1024), pg, ch.reshape(8, 32, 1024)


def solution(mesh):
    rows = P("node", "tile", None)
    placed = (rows, P("node"), P("node"), P(), P(), P("node", "tile"), P("node", None), rows, P("node", "tile"))
    return jax.shard_map(
        on_device, mesh=mesh, in_specs=placed, out_specs=(rows, rows, rows), check_vma=False
    )
```

```python
import functools

import jax
import jax.numpy as jnp
from jax import lax
from jax.experimental import pallas as pl
from jax.experimental.pallas import tpu as pltpu
from jax.sharding import PartitionSpec as P

F32, BF16 = jnp.float32, jnp.bfloat16
MESH = pl.DeviceIdType.MESH


def split(v):
    high = v.astype(BF16)
    return high, (v - high.astype(F32)).astype(BF16)


def mm(a, b, dims=((1,), (0,))):
    return lax.dot_general(a, b, (dims, ((), ())), preferred_element_type=F32)


def mm2(a, b, dims=((1,), (0,))):
    return mm(a[0], b, dims) + mm(a[1], b, dims)


def mm3(a, b, dims=((1,), (0,))):
    return mm(a[0], b[0], dims) + (mm(a[0], b[1], dims) + mm(a[1], b[0], dims))


def total(terms):
    while len(terms) > 1:
        terms = [
            terms[i] + terms[i + 1] if i + 1 < len(terms) else terms[i]
            for i in range(0, len(terms), 2)
        ]
    return terms[0]


def small_inverse(d):
    b = len(d)
    if b == 2:
        r = 1.0 / (d[0][0] * d[1][1] - d[0][1] * d[0][1])
        off = -d[0][1] * r
        return [[d[1][1] * r, off], [off, d[0][0] * r]]
    h = b // 2
    span = range(h)
    x = small_inverse([[d[i][j] for j in span] for i in span])
    y = [[d[i][h + j] for j in span] for i in span]
    w = [[total([x[i][k] * y[k][j] for k in span]) for j in span] for i in span]
    s = [[None] * h for _ in span]
    for i in span:
        for j in range(i, h):
            s[i][j] = s[j][i] = d[h + i][h + j] - total([y[k][i] * w[k][j] for k in span])
    q = small_inverse(s)
    wq = [[total([w[i][k] * q[k][j] for k in span]) for j in span] for i in span]
    out = [[None] * b for _ in range(b)]
    for i in span:
        for j in range(i, h):
            out[i][j] = out[j][i] = x[i][j] + total([wq[i][k] * w[j][k] for k in span])
        for j in span:
            out[i][h + j] = out[h + j][i] = -wq[i][j]
            out[h + i][h + j] = q[i][j]
    return out


def sweep(a, trips, beside=None, b=4, unroll=8):
    n = a.shape[0]
    lane = lax.broadcasted_iota(jnp.int32, (1, n), 1)
    lanes = lax.broadcasted_iota(jnp.int32, (n, n), 1)
    sub = lax.broadcasted_iota(jnp.int32, (n, 1), 0)

    def body(trip, a):
        if beside is not None:
            beside(trip)
        for low in range(0, unroll, b):
            ks = range(low, low + b)
            d = [[jnp.broadcast_to(a[i : i + 1, j : j + 1], (1, n)) for j in ks] for i in ks]
            inv = small_inverse(d)
            rows = [a[j : j + 1, :] for j in ks]
            in_rows = (sub >= low) & (sub < low + b)
            cols = [jnp.where(sub == k, -1.0, jnp.where(in_rows, 0.0, a[:, k : k + 1])) for k in ks]
            new = []
            for i in range(b):
                t = total([inv[i][j] * rows[j] for j in range(b)])
                for j in range(b):
                    t = jnp.where(lane == low + j, inv[i][j], t)
                new.append(t)
            a = jnp.where(((lanes >= low) & (lanes < low + b)) | in_rows, 0.0, a)
            for i in range(b):
                a = a - cols[i] * new[i]
        a = jnp.concatenate([a[unroll:], a[:unroll]], axis=0)
        return pltpu.roll(a, n - unroll, 1)

    return lax.fori_loop(0, trips, body, a)


ORDER = (0, 1, 3, 2)
HOPS = ((4, 3, 3, 4), (3, 4, 4, 3))
BLOCKS = 5


def place():
    n, t = lax.axis_index("node"), lax.axis_index("tile")
    return lax.rem(n, 2), n // 2, t // 4, lax.rem(t, 4)


def kernel(
    cw, po, cc, a_in, b_in, iw_in, pcov_in,
    pcr_out, pgr_out, spr_out,
    ccv, a5, b5, at5, lt, e5, p5, acc, mine, theirs, wt, wr, iw, iwr, pcov, pk, eb,
    bh, bl, cpl, gv, gh, gl, cl2, mom, pcv, pcr, pgr, spv, spr,
    load_sem, loc_sem, out_sem, sa_s, sa_r, sb_s, sb_r, pa_s, pa_r,
    er_s, er_r, ef_s, ef_r, pr_s, pr_r, pf_s, pf_r,
    gs_s, gs_r, cs_s, cs_r, ss_s, ss_r, sf_s, sf_r,
):
    c, y, z, x = place()
    oc = 1 - c
    own, jq = x // 2, lax.rem(x, 2)

    def dev(core, zz, xx):
        return (2 * y + core, 4 * zz + xx)

    def xs(dx):
        return lax.rem(x + dx + 4, 4)

    def zs(dz):
        return lax.rem(z + dz + 8, 8)

    def remote(src, dst, ssem, rsem, where):
        return pltpu.make_async_remote_copy(
            src_ref=src, dst_ref=dst, send_sem=ssem, recv_sem=rsem,
            device_id=where, device_id_type=MESH,
        )

    def lanes(block):
        return pl.ds(pl.multiple_of(lax.rem(block, 8) * 128, 128), 128)

    barrier = pltpu.get_barrier_semaphore()
    for dx in range(4):
        for core in ((oc,) if dx == 0 else (c, oc)):
            pl.semaphore_signal(barrier, inc=1, device_id=dev(core, z, xs(dx)), device_id_type=MESH)
    for dz in (1, -1):
        pl.semaphore_signal(barrier, inc=1, device_id=dev(c, zs(dz), x), device_id_type=MESH)

    loads = [
        pltpu.make_async_copy(cc, ccv, load_sem.at[0]),
        pltpu.make_async_copy(b_in, b5, load_sem.at[1]),
        pltpu.make_async_copy(a_in, a5, load_sem.at[2]),
        pltpu.make_async_copy(iw_in, iw, load_sem.at[3]),
        pltpu.make_async_copy(pcov_in, pcov, load_sem.at[4]),
    ]
    for cp in loads:
        cp.start()

    first = 4 * y
    coef = [
        [jnp.where(po[k] == first + q, cw[k].astype(F32), 0.0) for q in range(4)]
        for k in range(8)
    ]
    sub8 = lax.broadcasted_iota(jnp.int32, (8, 128), 0)
    tile = jnp.zeros((8, 128), F32)
    for q in range(4):
        s = total([coef[k][q] for k in range(8)])
        tile = jnp.where(sub8 == q, s, tile)
    wt[...] = tile

    loads[0].wait()

    def weigh(i, _):
        cols = pl.ds(pl.multiple_of(i * 256, 256), 256)
        for h in range(2):
            sums = [None] * 4
            for k in range(8):
                v = ccv[k, 16 * h : 16 * h + 16, cols]
                for q in range(4):
                    term = coef[k][q] * v
                    sums[q] = term if k == 0 else sums[q] + term
            for q in range(4):
                mine[q, h, :, cols] = sums[q]
        return 0

    lax.fori_loop(0, 4, weigh, 0)

    loads[3].wait()
    pl.semaphore_wait(barrier, 9)

    pair = dev(oc, z, x)
    swap = [
        remote(mine.at[:, oc], theirs, sa_s.at[0], sa_r.at[0], pair),
        remote(wt, wr, sa_s.at[1], sa_r.at[1], pair),
        remote(iw, iwr, sa_s.at[2], sa_r.at[2], pair),
    ]
    for cp in swap:
        cp.start()

    loads[1].wait()
    lt[0:256, 0:1024] = b5[...].reshape(1024, 256).T
    loads[2].wait()

    def turn(i, _):
        block = a5[pl.ds(i, 1)].reshape(128, 1024)
        at5[:, :, :, :, pl.ds(pl.multiple_of(i * 128, 128), 128)] = block.T.reshape(8, 4, 2, 16, 128)
        return 0

    lax.fori_loop(0, 8, turn, 0)
    lt[256:320, 0:1024] = at5[z, :, c].reshape(64, 1024)
    lt[:, 1024:1536] = lt[:, 0:512]
    loads[4].wait()
    for p in range(BLOCKS):
        pk[:, :, 128 * p : 128 * p + 128] = pcov[:, :, lanes(z + p)]

    for cp in swap:
        cp.wait_recv()
    wsum = wt[...] + wr[...]
    for q in range(4):
        w = wsum[q : q + 1, 0:1]
        for p in range(BLOCKS):
            e = (mine[q, c, :, lanes(z + p)] + theirs[q, :, lanes(z + p)]) / w
            high = e.astype(BF16)
            eb[q, :, 128 * p : 128 * p + 128] = high
            if p == 0:
                eb[q, :, 128 * BLOCKS :] = (e - high.astype(F32)).astype(BF16)

    spread_e = [
        remote(eb.at[xs(dx)], e5.at[z, x, c], sb_s.at[dx], sb_r.at[dx], dev(c, z, xs(dx)))
        for dx in (2, 1, 3)
    ]
    for cp in spread_e:
        cp.start()
    e5[z, x, c] = eb[x]

    def cov_copy(dx, other):
        q = xs(dx)
        core = oc if other else c
        return remote(
            pk.at[lax.rem(q, 2), pl.ds(pl.multiple_of(16 * core, 16), 16)],
            p5.at[z, x, core], pa_s.at[dx, int(other)], pa_r.at[dx], dev(core, z, q),
        )

    def cov_local():
        return pltpu.make_async_copy(
            pk.at[jq, pl.ds(pl.multiple_of(16 * c, 16), 16)], p5.at[z, x, c], loc_sem.at[0]
        )

    def cov_start():
        for dx in (2, 1, 3, 0):
            @pl.when(xs(dx) // 2 == c)
            def _(dx=dx):
                cov_copy(dx, True).start()
                (cov_copy(dx, False) if dx else cov_local()).start()

    def cov_wait():
        for dx in (2, 1, 3):
            remote(pk.at[0, 0:16], p5.at[z, xs(-dx), c], pa_s.at[dx, 0], pa_r.at[dx], pair).wait_recv()

        @pl.when(own == c)
        def _():
            cov_local().wait()

        @pl.when(own != c)
        def _():
            remote(pk.at[0, 0:16], p5.at[z, x, c], pa_s.at[0, 0], pa_r.at[0], pair).wait_recv()

    def ring(buf, ssem, rsem, d, s, h, got):
        sign = 1 - 2 * d
        part = buf.at[zs(-sign * (s if got else s - 1)), xs(-h), c]
        return remote(part, part, ssem.at[d, s - 1, h], rsem.at[d, s - 1, h], dev(c, zs(sign), x))

    def hand(buf, fs, fr, d, s, h, core):
        sign = 1 - 2 * d
        part = buf.at[zs(-sign * s), xs(-h), core]
        return remote(part, part, fs.at[d, s, h], fr.at[d, s, h], pair)

    def ring_start(buf, ssem, rsem, fs, fr, h):
        for d in (0, 1):
            ring(buf, ssem, rsem, d, 1, h, False).start()
        hand(buf, fs, fr, 0, 0, h, c).start()

    def ring_step(buf, ssem, rsem, fs, fr, s, pieces=ORDER):
        for h in pieces:
            for d in (0, 1):
                if s <= HOPS[d][h]:
                    ring(buf, ssem, rsem, d, s, h, True).wait_recv()
                    if s < HOPS[d][h]:
                        ring(buf, ssem, rsem, d, s + 1, h, False).start()
                    hand(buf, fs, fr, d, s, h, c).start()

    def hand_wait(buf, fs, fr, s):
        for h in ORDER:
            for d in (0,) if s == 0 else (0, 1):
                if s <= HOPS[d][h]:
                    hand(buf, fs, fr, d, s, h, oc).wait_recv()

    def drain(buf, ssem, rsem, fs, fr):
        for h in ORDER:
            hand(buf, fs, fr, 0, 0, h, c).wait_send()
            for d in range(2):
                for s in range(1, HOPS[d][h] + 1):
                    ring(buf, ssem, rsem, d, s, h, False).wait_send()
                    hand(buf, fs, fr, d, s, h, c).wait_send()

    e_ring = (e5, er_s, er_r, ef_s, ef_r)
    p_ring = (p5, pr_s, pr_r, pf_s, pf_r)

    def chunk_add(buf, zc, left2, out):
        left = left2[:, lanes(zc)]
        chunk = buf[zc].reshape(128, buf.shape[-1])
        for p in range(BLOCKS):
            v = mm(left, chunk[:, 128 * p : 128 * p + 128])
            if p == 0 and buf.shape[-1] > 128 * BLOCKS:
                v = v + mm(left, chunk[:, 128 * BLOCKS :])
            out[:, lanes(zc + p)] += v
        turned = left2[:, pl.ds(pl.multiple_of(128 * zc + 128, 128), 384)]
        out[:, lanes(zc)] += mm(turned, chunk[:, 128:512], ((1,), (1,)))

    ring_start(*e_ring, 0)
    acc[...] = jnp.zeros_like(acc)
    for dx in ORDER[1:]:
        remote(eb.at[xs(dx)], e5.at[z, xs(-dx), c], sb_s.at[dx], sb_r.at[dx], dev(c, z, xs(dx))).wait_recv()
        ring_start(*e_ring, dx)
    cov_start()
    for s in range(1, 5):
        ring_step(*e_ring, s, ORDER[:2])
        hand_wait(e5, ef_s, ef_r, s - 1)
        chunk_add(e5, zs(1 - s), lt, acc)
        ring_step(*e_ring, s, ORDER[2:])
        if s > 1:
            chunk_add(e5, zs(s - 1), lt, acc)
    cov_wait()
    for h in ORDER:
        ring_start(*p_ring, h)
    hand_wait(e5, ef_s, ef_r, 4)
    chunk_add(e5, zs(4), lt, acc)

    hi, lo = split(acc[...])
    bh[...] = hi
    bl[...] = lo
    bfull = b5[...].reshape(1024, 256)
    small = mm(bh[...], bfull) + mm(bl[...], bfull)
    weights = jnp.where(own == c, iw[pl.ds(jq, 1), :], iwr[pl.ds(jq, 1), :])
    r256 = lax.broadcasted_iota(jnp.int32, (256, 256), 0)
    c256 = lax.broadcasted_iota(jnp.int32, (256, 256), 1)
    curv = small[0:256] + jnp.where(r256 == c256, weights, 0.0)
    cpl_own = split(small[256:320])

    def times_a(trip):
        rows = pl.ds(pl.multiple_of(lax.rem(trip, 2) * 160, 32), 160)
        cols = pl.ds(pl.multiple_of((trip // 2) * 256, 256), 256)
        right = a5[:, :, :, :, cols].reshape(1024, 256)
        cpl[rows, cols] = mm(bh[rows, :], right) + mm(bl[rows, :], right)

    s11, s12, s22 = curv[:128, :128], curv[:128, 128:], curv[128:, 128:]
    inv = sweep(s11, 8, times_a)
    ring_step(*p_ring, 1)
    inv = sweep(inv, 8)
    ring_step(*p_ring, 2)
    inv_s, s12_s = split(inv), split(s12)
    w = mm3(inv_s, s12_s)
    w_s = split(w)
    inv2 = sweep(s22 - mm3(s12_s, w_s, ((0,), (0,))), 8)
    ring_step(*p_ring, 3)
    inv2 = sweep(inv2, 8)
    ring_step(*p_ring, 4)
    wq = mm3(w_s, split(inv2))
    inv1 = inv + mm3(split(wq), w_s, ((1,), (1,)))
    full_s = split(
        jnp.concatenate(
            [jnp.concatenate([inv1, -wq], axis=1), jnp.concatenate([-wq.T, inv2], axis=1)], axis=0
        )
    )

    def back(i, _):
        cols = pl.ds(pl.multiple_of(i * 256, 256), 256)
        g = mm3(full_s, split(cpl[0:256, cols]))
        gv[:, cols] = g
        gh[:, cols], gl[:, cols] = split(g)
        return 0

    lax.fori_loop(0, 4, back, 0)

    def gain_copy(dx):
        xx = xs(dx)
        rows = pl.ds(pl.multiple_of(32 * z + 8 * xx, 8), 8)
        return remote(gv.at[rows], pgr.at[jq], gs_s.at[dx], gs_r.at[dx], dev(c, z, xx))

    @pl.when(own == c)
    def _():
        for dx in (2, 1, 3):
            gain_copy(dx).start()
        pgr[jq] = gv[pl.ds(pl.multiple_of(32 * z + 8 * x, 8), 8), :]

    def cost(i, _):
        cols = pl.ds(pl.multiple_of(i * 256, 256), 256)
        v = cpl[256:320, cols] - mm3(cpl_own, (gh[:, cols], gl[:, cols]))
        pcv[:, :, cols] = v.reshape(4, 16, 256)
        return 0

    lax.fori_loop(0, 4, cost, 0)

    def cost_copy(dx):
        return remote(pcv.at[xs(dx)], pcr.at[jq, c], cs_s.at[dx], cs_r.at[dx, c], dev(own, z, xs(dx)))

    for dx in (2, 1, 3):
        cost_copy(dx).start()

    @pl.when(own == c)
    def _():
        pcr[jq, c] = pcv[x]

    @pl.when(own != c)
    def _():
        cost_copy(0).start()

    a_rows = a5[z, :, c].reshape(64, 1024).astype(F32)
    b_rows = b5[z, :, c].reshape(64, 256)
    closed = (a_rows - (mm(b_rows, gh[...]) + mm(b_rows, gl[...]))).astype(BF16)
    cl2[:, 0:1024] = closed
    cl2[:, 1024:1536] = closed[:, 0:512]
    mom[...] = jnp.zeros_like(mom)
    for s in range(5):
        hand_wait(p5, pf_s, pf_r, s)

    def moment(i, _):
        chunk_add(p5, i, cl2, mom)
        return 0

    lax.fori_loop(0, 8, moment, 0)
    moment_s = split(mom[...])
    nt = ((1,), (1,))
    inner_s = split(mm3(moment_s, (gh[...], gl[...]), nt))

    def out_cols(i, _):
        cols = pl.ds(pl.multiple_of(i * 256, 256), 256)
        v = mm2(moment_s, at5[:, :, :, :, cols].reshape(1024, 256)) - mm2(inner_s, lt[0:256, cols])
        spv[:, :, cols] = v.reshape(4, 16, 256)
        return 0

    lax.fori_loop(0, 4, out_cols, 0)

    def spread_copy(dx):
        return remote(spv.at[xs(dx)], spr.at[x, c], ss_s.at[dx], ss_r.at[dx], dev(c, z, xs(dx)))

    def spread_got(dx):
        return remote(spv.at[xs(dx)], spr.at[xs(-dx), c], ss_s.at[dx], ss_r.at[dx], dev(c, z, xs(dx)))

    def spread_hand(dx, core):
        return remote(spr.at[xs(-dx), core], spr.at[xs(-dx), core], sf_s.at[dx], sf_r.at[dx], pair)

    for dx in (2, 1, 3):
        spread_copy(dx).start()
    spr[x, c] = spv[x]
    spread_hand(0, c).start()

    for dx in (1, 2, 3):
        @pl.when(xs(-dx) // 2 == c)
        def _(dx=dx):
            remote(gv.at[0:8], pgr.at[lax.rem(xs(-dx), 2)], gs_s.at[dx], gs_r.at[dx], pair).wait_recv()
            for core in range(2):
                remote(pcv.at[0], pcr.at[lax.rem(xs(-dx), 2), core], cs_s.at[dx], cs_r.at[dx, core], pair).wait_recv()

    @pl.when(own == c)
    def _():
        remote(pcv.at[0], pcr.at[jq, oc], cs_s.at[0], cs_r.at[0, oc], pair).wait_recv()

    out_pg = pltpu.make_async_copy(pgr, pgr_out, out_sem.at[0])
    out_pg.start()
    out_pc = pltpu.make_async_copy(pcr, pcr_out, out_sem.at[1])
    out_pc.start()

    for dx in (1, 3, 2):
        spread_got(dx).wait_recv()
        spread_hand(dx, c).start()
    for dx in range(4):
        spread_hand(dx, oc).wait_recv()

    out_sp = pltpu.make_async_copy(spr, spr_out, out_sem.at[2])
    out_sp.start()

    for cp in swap + spread_e:
        cp.wait_send()
    for dx in range(4):
        @pl.when(xs(dx) // 2 == c)
        def _(dx=dx):
            cov_copy(dx, True).wait_send()
            if dx:
                cov_copy(dx, False).wait_send()
    drain(*e_ring)
    drain(*p_ring)

    @pl.when(own == c)
    def _():
        for dx in (2, 1, 3):
            gain_copy(dx).wait_send()

    @pl.when(own != c)
    def _():
        cost_copy(0).wait_send()

    for dx in (2, 1, 3):
        cost_copy(dx).wait_send()
        spread_copy(dx).wait_send()
    for dx in range(4):
        spread_hand(dx, c).wait_send()
    out_pg.wait()
    out_pc.wait()
    out_sp.wait()


def finish(po, sw, nz, pcr, pgr, spr, pc, pg, ch):
    c, y, z, x = place()
    zlane = pl.ds(pl.multiple_of(z * 128, 128), 128)
    diag = lax.broadcasted_iota(jnp.int32, (32, 128), 1) == (
        32 * x + lax.broadcasted_iota(jnp.int32, (32, 128), 0)
    )
    pick = lax.broadcasted_iota(jnp.int32, (32, 32), 1) == lax.broadcasted_iota(jnp.int32, (32, 32), 0)

    def on_diag(row):
        column = jnp.sum(jnp.where(pick, row, 0.0), axis=1, keepdims=True)
        return jnp.where(diag, column, 0.0).reshape(2, 16, 128)

    pg[...] = pgr[...]
    pc[...] = pcr[...]
    for j in range(2):
        pc[j, :, :, zlane] += on_diag(sw[j : j + 1, :])
    for k in range(8):
        parent = [po[k] == 4 * y + q for q in range(4)]

        def fill(i, _):
            cols = pl.ds(pl.multiple_of(i * 256, 256), 256)
            v = spr[0, :, :, cols]
            for q in range(1, 4):
                v = jnp.where(parent[q], spr[q, :, :, cols], v)
            ch[k, :, :, cols] = v
            return 0

        lax.fori_loop(0, 4, fill, 0)
        ch[k, :, :, zlane] += on_diag(nz[k : k + 1, :])


def on_device(cc, cw, po, a, b, sw, iw, pcov, nz):
    any_, vmem, smem = (pl.BlockSpec(memory_space=m) for m in (pl.ANY, pltpu.VMEM, pltpu.SMEM))
    v, dma = pltpu.VMEM, pltpu.SemaphoreType.DMA
    scratch = [
        v((8, 32, 1024), F32),
        v((8, 4, 2, 16, 1024), BF16),
        v((8, 4, 2, 16, 256), BF16),
        v((8, 4, 2, 16, 1024), BF16),
        v((320, 1536), BF16),
        v((8, 4, 2, 16, 128 * BLOCKS + 128), BF16),
        v((8, 4, 2, 16, 128 * BLOCKS), BF16),
        v((320, 1024), F32),
        v((4, 2, 16, 1024), F32),
        v((4, 16, 1024), F32),
        v((8, 128), F32),
        v((8, 128), F32),
        v((2, 256), F32),
        v((2, 256), F32),
        v((2, 32, 1024), BF16),
        v((2, 32, 128 * BLOCKS), BF16),
        v((4, 16, 128 * BLOCKS + 128), BF16),
        v((320, 1024), BF16),
        v((320, 1024), BF16),
        v((320, 1024), F32),
        v((256, 1024), F32),
        v((256, 1024), BF16),
        v((256, 1024), BF16),
        v((64, 1536), BF16),
        v((64, 1024), F32),
        v((4, 16, 1024), F32),
        v((2, 2, 16, 1024), F32),
        v((2, 8, 1024), F32),
        v((4, 16, 1024), F32),
        v((4, 2, 16, 1024), F32),
        dma((5,)), dma((1,)), dma((3,)),
        dma((3,)), dma((3,)),
        dma((4,)), dma((4,)),
        dma((4, 2)), dma((4,)),
        dma((2, 4, 4)), dma((2, 4, 4)), dma((2, 5, 4)), dma((2, 5, 4)),
        dma((2, 4, 4)), dma((2, 4, 4)), dma((2, 5, 4)), dma((2, 5, 4)),
        dma((4,)), dma((4,)),
        dma((4,)), dma((4, 2)),
        dma((4,)), dma((4,)), dma((4,)), dma((4,)),
    ]
    pcr, pgr, spr = pl.pallas_call(
        kernel,
        out_shape=(
            jax.ShapeDtypeStruct((2, 2, 16, 1024), F32),
            jax.ShapeDtypeStruct((2, 8, 1024), F32),
            jax.ShapeDtypeStruct((4, 2, 16, 1024), F32),
        ),
        in_specs=[smem, smem, any_, any_, any_, any_, any_],
        out_specs=(any_, any_, any_),
        scratch_shapes=scratch,
        compiler_params=pltpu.CompilerParams(collective_id=0, has_side_effects=True),
    )(cw, po, cc, a.reshape(8, 4, 2, 16, 1024), b.reshape(8, 4, 2, 16, 256), iw, pcov)
    pc, pg, ch = pl.pallas_call(
        finish,
        out_shape=(
            jax.ShapeDtypeStruct((2, 2, 16, 1024), F32),
            jax.ShapeDtypeStruct((2, 8, 1024), F32),
            jax.ShapeDtypeStruct((8, 2, 16, 1024), F32),
        ),
        in_specs=[smem] + [vmem] * 5,
        out_specs=(vmem, vmem, vmem),
    )(po, sw, nz, pcr, pgr, spr)
    return pc.reshape(2, 32, 1024), pg, ch.reshape(8, 32, 1024)


def solution(mesh):
    rows = P("node", "tile", None)
    placed = (rows, P("node"), P("node"), P(), P(), P("node", "tile"), P("node", None), rows, P("node", "tile"))
    return jax.shard_map(
        on_device, mesh=mesh, in_specs=placed, out_specs=(rows, rows, rows), check_vma=False
    )
```

```python
import functools

import jax
import jax.numpy as jnp
from jax import lax
from jax.experimental import pallas as pl
from jax.experimental.pallas import tpu as pltpu
from jax.sharding import PartitionSpec as P

F32, BF16 = jnp.float32, jnp.bfloat16
MESH = pl.DeviceIdType.MESH


def split(v):
    high = v.astype(BF16)
    return high, (v - high.astype(F32)).astype(BF16)


def mm(a, b, dims=((1,), (0,))):
    return lax.dot_general(a, b, (dims, ((), ())), preferred_element_type=F32)


def mm2(a, b, dims=((1,), (0,))):
    return mm(a[0], b, dims) + mm(a[1], b, dims)


def mm3(a, b, dims=((1,), (0,))):
    return mm(a[0], b[0], dims) + (mm(a[0], b[1], dims) + mm(a[1], b[0], dims))


def total(terms):
    while len(terms) > 1:
        terms = [
            terms[i] + terms[i + 1] if i + 1 < len(terms) else terms[i]
            for i in range(0, len(terms), 2)
        ]
    return terms[0]


def small_inverse(d):
    b = len(d)
    if b == 2:
        r = 1.0 / (d[0][0] * d[1][1] - d[0][1] * d[0][1])
        off = -d[0][1] * r
        return [[d[1][1] * r, off], [off, d[0][0] * r]]
    h = b // 2
    span = range(h)
    x = small_inverse([[d[i][j] for j in span] for i in span])
    y = [[d[i][h + j] for j in span] for i in span]
    w = [[total([x[i][k] * y[k][j] for k in span]) for j in span] for i in span]
    s = [[None] * h for _ in span]
    for i in span:
        for j in range(i, h):
            s[i][j] = s[j][i] = d[h + i][h + j] - total([y[k][i] * w[k][j] for k in span])
    q = small_inverse(s)
    wq = [[total([w[i][k] * q[k][j] for k in span]) for j in span] for i in span]
    out = [[None] * b for _ in range(b)]
    for i in span:
        for j in range(i, h):
            out[i][j] = out[j][i] = x[i][j] + total([wq[i][k] * w[j][k] for k in span])
        for j in span:
            out[i][h + j] = out[h + j][i] = -wq[i][j]
            out[h + i][h + j] = q[i][j]
    return out


def sweep(a, trips, beside=None, b=4, unroll=32):
    n = a.shape[0]
    lane = lax.broadcasted_iota(jnp.int32, (1, n), 1)
    lanes = lax.broadcasted_iota(jnp.int32, (n, n), 1)
    sub = lax.broadcasted_iota(jnp.int32, (n, 1), 0)

    def body(trip, a):
        if beside is not None:
            beside(trip)
        for low in range(0, unroll, b):
            ks = range(low, low + b)
            d = [[jnp.broadcast_to(a[i : i + 1, j : j + 1], (1, n)) for j in ks] for i in ks]
            inv = small_inverse(d)
            rows = [a[j : j + 1, :] for j in ks]
            in_rows = (sub >= low) & (sub < low + b)
            cols = [jnp.where(sub == k, -1.0, jnp.where(in_rows, 0.0, a[:, k : k + 1])) for k in ks]
            new = []
            for i in range(b):
                t = total([inv[i][j] * rows[j] for j in range(b)])
                for j in range(b):
                    t = jnp.where(lane == low + j, inv[i][j], t)
                new.append(t)
            a = jnp.where(((lanes >= low) & (lanes < low + b)) | in_rows, 0.0, a)
            for i in range(b):
                a = a - cols[i] * new[i]
        a = jnp.concatenate([a[unroll:], a[:unroll]], axis=0)
        return pltpu.roll(a, n - unroll, 1)

    return lax.fori_loop(0, trips, body, a)


ORDER = (0, 1, 3, 2)
HOPS = ((4, 3, 3, 4), (3, 4, 4, 3))
NEAR = (1, -1, 2, -2, 3, -3)
BLOCKS = 5


def place():
    n, t = lax.axis_index("node"), lax.axis_index("tile")
    return lax.rem(n, 2), n // 2, t // 4, lax.rem(t, 4)


def kernel(
    cw_in, po_in, cc, a_in, b_in, iw_in, pcov_in,
    pcr_out, pgr_out, spr_out,
    ccv, a5, b5, at5, lt, e5, p5, acc, mine, theirs, wt, wr, iw, iwr, pcov, pk, eb,
    bh, bl, cpl, gv, gh, gl, cl2, mom, pcv, pcr, pgr, spv, spr, cost_via, spread_via, cw, po,
    load_sem, loc_sem, out_sem, sa_s, sa_r, sb_s, sb_r, pa_s, pa_r,
    er_s, er_r, ef_s, ef_r, pr_s, pr_r, pf_s, pf_r, far_s, far_r,
    gs_s, gs_r, cs_s, cs_r, ss_s, ss_r, sf_s, sf_r, via_s, via_r, on_s,
):
    c, y, z, x = place()
    oc = 1 - c
    own, jq = x // 2, lax.rem(x, 2)

    def dev(core, zz, xx):
        return (2 * y + core, 4 * zz + xx)

    def xs(dx):
        return lax.rem(x + dx + 4, 4)

    def zs(dz):
        return lax.rem(z + dz + 8, 8)

    def remote(src, dst, ssem, rsem, where):
        return pltpu.make_async_remote_copy(
            src_ref=src, dst_ref=dst, send_sem=ssem, recv_sem=rsem,
            device_id=where, device_id_type=MESH,
        )

    def lanes(block):
        return pl.ds(pl.multiple_of(lax.rem(block, 8) * 128, 128), 128)

    barrier = pltpu.get_barrier_semaphore()
    for dx in range(4):
        for core in ((oc,) if dx == 0 else (c, oc)):
            pl.semaphore_signal(barrier, inc=1, device_id=dev(core, z, xs(dx)), device_id_type=MESH)
    for dz in range(1, 8):
        pl.semaphore_signal(barrier, inc=1, device_id=dev(c, zs(dz), x), device_id_type=MESH)

    loads = [
        pltpu.make_async_copy(cc, ccv, load_sem.at[0]),
        pltpu.make_async_copy(b_in, b5, load_sem.at[1]),
        pltpu.make_async_copy(a_in, a5, load_sem.at[2]),
        pltpu.make_async_copy(iw_in, iw, load_sem.at[3]),
        pltpu.make_async_copy(pcov_in, pcov, load_sem.at[4]),
        pltpu.make_async_copy(cw_in, cw, load_sem.at[5]),
        pltpu.make_async_copy(po_in, po, load_sem.at[6]),
    ]
    for i in (5, 6, 0, 1, 2, 3, 4):
        loads[i].start()
    loads[5].wait()
    loads[6].wait()

    first = 4 * y
    coef = [
        [jnp.where(po[k] == first + q, cw[k].astype(F32), 0.0) for q in range(4)]
        for k in range(8)
    ]
    sub8 = lax.broadcasted_iota(jnp.int32, (8, 128), 0)
    tile = jnp.zeros((8, 128), F32)
    for q in range(4):
        s = total([coef[k][q] for k in range(8)])
        tile = jnp.where(sub8 == q, s, tile)
    wt[...] = tile

    loads[0].wait()

    def weigh(i, _):
        cols = pl.ds(pl.multiple_of(i * 256, 256), 256)
        for h in range(2):
            sums = [None] * 4
            for k in range(8):
                v = ccv[k, 16 * h : 16 * h + 16, cols]
                for q in range(4):
                    term = coef[k][q] * v
                    sums[q] = term if k == 0 else sums[q] + term
            for q in range(4):
                mine[q, h, :, cols] = sums[q]
        return 0

    lax.fori_loop(0, 4, weigh, 0)

    loads[3].wait()
    pl.semaphore_wait(barrier, 14)

    pair = dev(oc, z, x)
    swap = [
        remote(mine.at[:, oc], theirs, sa_s.at[0], sa_r.at[0], pair),
        remote(wt, wr, sa_s.at[1], sa_r.at[1], pair),
        remote(iw, iwr, sa_s.at[2], sa_r.at[2], pair),
    ]
    for cp in swap:
        cp.start()

    for cp in swap:
        cp.wait_recv()
    wsum = wt[...] + wr[...]
    for q in range(4):
        w = wsum[q : q + 1, 0:1]
        for p in range(BLOCKS):
            e = (mine[q, c, :, lanes(z + p)] + theirs[q, :, lanes(z + p)]) / w
            high = e.astype(BF16)
            eb[q, :, 128 * p : 128 * p + 128] = high
            if p == 0:
                eb[q, :, 128 * BLOCKS :] = (e - high.astype(F32)).astype(BF16)

    spread_e = [
        remote(eb.at[xs(dx)], e5.at[z, x, c], sb_s.at[dx], sb_r.at[dx], dev(c, z, xs(dx)))
        for dx in (2, 1, 3)
    ]
    for cp in spread_e:
        cp.start()
    e5[z, x, c] = eb[x]

    def cov_copy(dx, other):
        q = xs(dx)
        core = oc if other else c
        return remote(
            pk.at[lax.rem(q, 2), pl.ds(pl.multiple_of(16 * core, 16), 16)],
            p5.at[z, x, core], pa_s.at[dx, int(other)], pa_r.at[dx], dev(core, z, q),
        )

    def cov_local():
        return pltpu.make_async_copy(
            pk.at[jq, pl.ds(pl.multiple_of(16 * c, 16), 16)], p5.at[z, x, c], loc_sem.at[0]
        )

    def cov_start():
        for dx in (2, 1, 3, 0):
            @pl.when(xs(dx) // 2 == c)
            def _(dx=dx):
                cov_copy(dx, True).start()
                (cov_copy(dx, False) if dx else cov_local()).start()

    def cov_wait():
        for dx in (2, 1, 3):
            remote(pk.at[0, 0:16], p5.at[z, xs(-dx), c], pa_s.at[dx, 0], pa_r.at[dx], pair).wait_recv()

        @pl.when(own == c)
        def _():
            cov_local().wait()

        @pl.when(own != c)
        def _():
            remote(pk.at[0, 0:16], p5.at[z, x, c], pa_s.at[0, 0], pa_r.at[0], pair).wait_recv()

    def ring(buf, ssem, rsem, d, s, h, got):
        sign = 1 - 2 * d
        part = buf.at[zs(-sign * (s if got else s - 1)), xs(-h), c]
        return remote(part, part, ssem.at[d, s - 1, h], rsem.at[d, s - 1, h], dev(c, zs(sign), x))

    def hand(buf, fs, fr, d, s, h, core):
        sign = 1 - 2 * d
        part = buf.at[zs(-sign * s), xs(-h), core]
        return remote(part, part, fs.at[d, s, h], fr.at[d, s, h], pair)

    def ring_start(buf, ssem, rsem, fs, fr, h):
        for d in (0, 1):
            ring(buf, ssem, rsem, d, 1, h, False).start()
        hand(buf, fs, fr, 0, 0, h, c).start()

    def ring_step(buf, ssem, rsem, fs, fr, s, pieces=ORDER):
        for h in pieces:
            for d in (0, 1):
                if s <= HOPS[d][h]:
                    ring(buf, ssem, rsem, d, s, h, True).wait_recv()
                    if s < HOPS[d][h]:
                        ring(buf, ssem, rsem, d, s + 1, h, False).start()
                    hand(buf, fs, fr, d, s, h, c).start()

    def hand_wait(buf, fs, fr, s):
        for h in ORDER:
            for d in (0,) if s == 0 else (0, 1):
                if s <= HOPS[d][h]:
                    hand(buf, fs, fr, d, s, h, oc).wait_recv()

    def drain(buf, ssem, rsem, fs, fr):
        for h in ORDER:
            hand(buf, fs, fr, 0, 0, h, c).wait_send()
            for d in range(2):
                for s in range(1, HOPS[d][h] + 1):
                    ring(buf, ssem, rsem, d, s, h, False).wait_send()
                    hand(buf, fs, fr, d, s, h, c).wait_send()

    e_ring = (e5, er_s, er_r, ef_s, ef_r)

    def cov_send(dz):
        part = p5.at[z, :, c]
        return remote(part, part, pr_s.at[dz + 3], pr_r.at[dz + 3], dev(c, zs(dz), x))

    def cov_got(dz):
        part = p5.at[zs(-dz), :, c]
        return remote(part, part, pr_s.at[dz + 3], pr_r.at[dz + 3], pair)

    def cov_hand(dz, core):
        part = p5.at[zs(-dz), :, core]
        return remote(part, part, pf_s.at[dz + 3], pf_r.at[dz + 3], pair)

    def cov_onward(d, got=False):
        sign = 1 - 2 * d
        part = p5.at[zs(4 if got else -3 * sign), pl.ds(2 * d, 2), c]
        return remote(part, part, far_s.at[d], far_r.at[d], dev(c, zs(sign), x))

    def cov_far_hand(d, core):
        part = p5.at[zs(4), pl.ds(2 * d, 2), core]
        return remote(part, part, far_s.at[2 + d], far_r.at[2 + d], pair)

    def cov_take(dz):
        cov_got(dz).wait_recv()
        cov_hand(dz, c).start()


    def chunk_add(buf, zc, left2, out):
        left = left2[:, lanes(zc)]
        chunk = buf[zc].reshape(128, buf.shape[-1])
        for p in range(BLOCKS):
            v = mm(left, chunk[:, 128 * p : 128 * p + 128])
            if p == 0 and buf.shape[-1] > 128 * BLOCKS:
                v = v + mm(left, chunk[:, 128 * BLOCKS :])
            out[:, lanes(zc + p)] += v
        turned = left2[:, pl.ds(pl.multiple_of(128 * zc + 128, 128), 384)]
        out[:, lanes(zc)] += mm(turned, chunk[:, 128:512], ((1,), (1,)))

    ring_start(*e_ring, 0)
    loads[1].wait()
    lt[0:256, 0:1024] = b5[...].reshape(1024, 256).T
    loads[2].wait()

    def turn(i, _):
        block = a5[pl.ds(i, 1)].reshape(128, 1024)
        at5[:, :, :, :, pl.ds(pl.multiple_of(i * 128, 128), 128)] = block.T.reshape(8, 4, 2, 16, 128)
        return 0

    lax.fori_loop(0, 8, turn, 0)
    lt[256:320, 0:1024] = at5[z, :, c].reshape(64, 1024)
    lt[:, 1024:1536] = lt[:, 0:512]
    loads[4].wait()
    for p in range(BLOCKS):
        pk[:, :, 128 * p : 128 * p + 128] = pcov[:, :, lanes(z + p)]
    acc[...] = jnp.zeros_like(acc)
    for dx in ORDER[1:]:
        remote(eb.at[xs(dx)], e5.at[z, xs(-dx), c], sb_s.at[dx], sb_r.at[dx], dev(c, z, xs(dx))).wait_recv()
        ring_start(*e_ring, dx)
    cov_start()
    ring_step(*e_ring, 1)
    hand_wait(e5, ef_s, ef_r, 0)
    chunk_add(e5, z, lt, acc)
    ring_step(*e_ring, 2)
    hand_wait(e5, ef_s, ef_r, 1)
    chunk_add(e5, zs(1), lt, acc)
    ring_step(*e_ring, 3)
    chunk_add(e5, zs(-1), lt, acc)
    hand_wait(e5, ef_s, ef_r, 2)
    chunk_add(e5, zs(2), lt, acc)
    chunk_add(e5, zs(-2), lt, acc)
    ring_step(*e_ring, 4)
    cov_wait()
    cov_hand(0, c).start()
    for dz in NEAR:
        cov_send(dz).start()
    hand_wait(e5, ef_s, ef_r, 3)
    chunk_add(e5, zs(3), lt, acc)
    chunk_add(e5, zs(-3), lt, acc)
    hand_wait(e5, ef_s, ef_r, 4)
    chunk_add(e5, zs(4), lt, acc)

    hi, lo = split(acc[...])
    bh[...] = hi
    bl[...] = lo
    bfull = b5[...].reshape(1024, 256)
    small = mm(bh[...], bfull) + mm(bl[...], bfull)
    weights = jnp.where(own == c, iw[pl.ds(jq, 1), :], iwr[pl.ds(jq, 1), :])
    r256 = lax.broadcasted_iota(jnp.int32, (256, 256), 0)
    c256 = lax.broadcasted_iota(jnp.int32, (256, 256), 1)
    curv = small[0:256] + jnp.where(r256 == c256, weights, 0.0)
    cpl_own = split(small[256:320])

    def times_a(trip):
        for part in range(2):
            cols = pl.ds(pl.multiple_of(trip * 512 + part * 256, 256), 256)
            right = a5[:, :, :, :, cols].reshape(1024, 256)
            cpl[:, cols] = mm(bh[...], right) + mm(bl[...], right)

    s11, s12, s22 = curv[:128, :128], curv[:128, 128:], curv[128:, 128:]
    inv = sweep(s11, 2, times_a)
    inv = sweep(inv, 2)
    cov_take(1)
    cov_take(-1)
    inv_s, s12_s = split(inv), split(s12)
    w = mm3(inv_s, s12_s)
    w_s = split(w)
    inv2 = sweep(s22 - mm3(s12_s, w_s, ((0,), (0,))), 2)
    for dz in (2, -2, 3, -3):
        cov_take(dz)
    for d in range(2):
        cov_onward(d).start()
    inv2 = sweep(inv2, 2)
    wq = mm3(w_s, split(inv2))
    inv1 = inv + mm3(split(wq), w_s, ((1,), (1,)))
    full_s = split(
        jnp.concatenate(
            [jnp.concatenate([inv1, -wq], axis=1), jnp.concatenate([-wq.T, inv2], axis=1)], axis=0
        )
    )

    def back(i, _):
        cols = pl.ds(pl.multiple_of(i * 256, 256), 256)
        g = mm3(full_s, split(cpl[0:256, cols]))
        gv[:, cols] = g
        gh[:, cols], gl[:, cols] = split(g)
        return 0

    lax.fori_loop(0, 4, back, 0)

    for d in range(2):
        cov_onward(d, True).wait_recv()
        cov_far_hand(d, c).start()

    def gain_copy(dx):
        xx = xs(dx)
        rows = pl.ds(pl.multiple_of(32 * z + 8 * xx, 8), 8)
        return remote(gv.at[rows], pgr.at[jq], gs_s.at[dx], gs_r.at[dx], dev(c, z, xx))

    @pl.when(own == c)
    def _():
        for dx in (2, 1, 3):
            gain_copy(dx).start()
        pgr[jq] = gv[pl.ds(pl.multiple_of(32 * z + 8 * x, 8), 8), :]

    def cost(i, _):
        cols = pl.ds(pl.multiple_of(i * 256, 256), 256)
        v = cpl[256:320, cols] - mm3(cpl_own, (gh[:, cols], gl[:, cols]))
        pcv[:, :, cols] = v.reshape(4, 16, 256)
        return 0

    lax.fori_loop(0, 4, cost, 0)

    def cost_copy(dx):
        return remote(pcv.at[xs(dx)], pcr.at[jq, c], cs_s.at[dx], cs_r.at[dx, c], dev(own, z, xs(dx)))

    way = 1 - 2 * c
    source = xs(-way)

    def cost_near():
        return remote(pcv.at[xs(2)], cost_via, via_s.at[0], via_r.at[0], dev(c, z, xs(way)))

    def cost_onward():
        return remote(
            cost_via, pcr.at[lax.rem(source, 2), c], on_s.at[0], cs_r.at[2, c], dev(source // 2, z, xs(way))
        )

    cost_near().start()
    for dx in (1, 3):
        cost_copy(dx).start()

    @pl.when(own == c)
    def _():
        pcr[jq, c] = pcv[x]

    @pl.when(own != c)
    def _():
        cost_copy(0).start()

    a_rows = a5[z, :, c].reshape(64, 1024).astype(F32)
    b_rows = b5[z, :, c].reshape(64, 256)
    closed = (a_rows - (mm(b_rows, gh[...]) + mm(b_rows, gl[...]))).astype(BF16)
    cl2[:, 0:1024] = closed
    cl2[:, 1024:1536] = closed[:, 0:512]
    for dz in (0,) + NEAR:
        cov_hand(dz, oc).wait_recv()
    for d in range(2):
        cov_far_hand(d, oc).wait_recv()
    nt = ((1,), (1,))
    for q in range(8):
        low = (q - BLOCKS + 1) % 8
        right = jnp.concatenate(
            [
                p5[(low + i) % 8, :, :, :, 128 * (BLOCKS - 1 - i) : 128 * (BLOCKS - i)].reshape(128, 128)
                for i in range(BLOCKS)
            ],
            axis=0,
        )
        mom[:, 128 * q : 128 * q + 128] = mm(cl2[:, 128 * low : 128 * (low + BLOCKS)], right) + mm(
            cl2[:, 128 * (q + 1) : 128 * (q + 4)], p5[q, :, :, :, 128:512].reshape(128, 384), nt
        )
    moment_s = split(mom[...])
    inner_s = split(mm3(moment_s, (gh[...], gl[...]), nt))

    cost_near().wait_recv()
    cost_onward().start()

    def spread_copy(dx, half):
        cols = pl.ds(512 * half, 512)
        return remote(
            spv.at[xs(dx), :, cols], spr.at[x, c, :, cols], ss_s.at[dx, half], ss_r.at[dx, half], dev(c, z, xs(dx))
        )

    def spread_got(dx, half):
        cols = pl.ds(512 * half, 512)
        return remote(
            spv.at[xs(dx), :, cols], spr.at[xs(-dx), c, :, cols], ss_s.at[dx, half], ss_r.at[dx, half], dev(c, z, xs(dx))
        )

    def spread_hand(dx, half, core):
        part = spr.at[xs(-dx), core, :, pl.ds(512 * half, 512)]
        return remote(part, part, sf_s.at[dx, half], sf_r.at[dx, half], pair)

    def spread_near(half):
        return remote(
            spv.at[xs(2), :, pl.ds(512 * half, 512)], spread_via.at[half],
            via_s.at[1 + half], via_r.at[1 + half], dev(c, z, xs(way)),
        )

    def spread_onward(half):
        return remote(
            spread_via.at[half], spr.at[source, c, :, pl.ds(512 * half, 512)],
            on_s.at[1 + half], ss_r.at[2, half], dev(c, z, xs(way)),
        )

    for half in range(2):
        for i in range(2):
            cols = slice(512 * half + 256 * i, 512 * half + 256 * i + 256)
            v = mm2(moment_s, at5[:, :, :, :, cols].reshape(1024, 256)) - mm2(inner_s, lt[0:256, cols])
            spv[:, :, cols] = v.reshape(4, 16, 256)

        spread_near(half).start()
        for dx in (1, 3):
            spread_copy(dx, half).start()
        cols = slice(512 * half, 512 * half + 512)
        spr[x, c, :, cols] = spv[x, :, cols]
        spread_hand(0, half, c).start()

    for half in range(2):
        spread_near(half).wait_recv()
        spread_onward(half).start()

    for cp in swap + spread_e:
        cp.wait_send()
    for dx in range(4):
        @pl.when(xs(dx) // 2 == c)
        def _(dx=dx):
            cov_copy(dx, True).wait_send()
            if dx:
                cov_copy(dx, False).wait_send()
    drain(*e_ring)
    cov_hand(0, c).wait_send()
    for dz in NEAR:
        cov_send(dz).wait_send()
        cov_hand(dz, c).wait_send()
    for d in range(2):
        cov_onward(d).wait_send()
        cov_far_hand(d, c).wait_send()

    for dx in (1, 2, 3):
        @pl.when(xs(-dx) // 2 == c)
        def _(dx=dx):
            remote(gv.at[0:8], pgr.at[lax.rem(xs(-dx), 2)], gs_s.at[dx], gs_r.at[dx], pair).wait_recv()
            for core in range(2):
                remote(pcv.at[0], pcr.at[lax.rem(xs(-dx), 2), core], cs_s.at[dx], cs_r.at[dx, core], pair).wait_recv()

    @pl.when(own == c)
    def _():
        remote(pcv.at[0], pcr.at[jq, oc], cs_s.at[0], cs_r.at[0, oc], pair).wait_recv()

    out_pg = pltpu.make_async_copy(pgr, pgr_out, out_sem.at[0])
    out_pg.start()
    out_pc = pltpu.make_async_copy(pcr, pcr_out, out_sem.at[1])
    out_pc.start()

    for half in range(2):
        for dx in (1, 3, 2):
            spread_got(dx, half).wait_recv()
            spread_hand(dx, half, c).start()
    out_own = pltpu.make_async_copy(spr.at[:, c], spr_out.at[:, c], out_sem.at[2])
    out_own.start()
    for half in range(2):
        for dx in range(4):
            spread_hand(dx, half, oc).wait_recv()
    out_pair = pltpu.make_async_copy(spr.at[:, oc], spr_out.at[:, oc], out_sem.at[3])
    out_pair.start()

    @pl.when(own == c)
    def _():
        for dx in (2, 1, 3):
            gain_copy(dx).wait_send()

    @pl.when(own != c)
    def _():
        cost_copy(0).wait_send()

    cost_near().wait_send()
    cost_onward().wait_send()
    for half in range(2):
        spread_near(half).wait_send()
        spread_onward(half).wait_send()
    for dx in (1, 3):
        cost_copy(dx).wait_send()
        for half in range(2):
            spread_copy(dx, half).wait_send()
    for half in range(2):
        for dx in range(4):
            spread_hand(dx, half, c).wait_send()
    out_pg.wait()
    out_pc.wait()
    out_own.wait()
    out_pair.wait()


def finish(po, sw, nz, pcr, pgr, spr, pc_out, pg_out, ch_out, pc, pg, ch, out_sem):
    outs = [
        pltpu.make_async_copy(pg, pg_out, out_sem.at[8]),
        pltpu.make_async_copy(pc, pc_out, out_sem.at[9]),
    ]
    c, y, z, x = place()
    zlane = pl.ds(pl.multiple_of(z * 128, 128), 128)
    diag = lax.broadcasted_iota(jnp.int32, (32, 128), 1) == (
        32 * x + lax.broadcasted_iota(jnp.int32, (32, 128), 0)
    )
    pick = lax.broadcasted_iota(jnp.int32, (32, 32), 1) == lax.broadcasted_iota(jnp.int32, (32, 32), 0)

    def on_diag(row):
        column = jnp.sum(jnp.where(pick, row, 0.0), axis=1, keepdims=True)
        return jnp.where(diag, column, 0.0).reshape(2, 16, 128)

    for k in range(8):
        parent = [po[k] == 4 * y + q for q in range(4)]

        def fill(i, _):
            cols = pl.ds(pl.multiple_of(i * 256, 256), 256)
            v = spr[0, :, :, cols]
            for q in range(1, 4):
                v = jnp.where(parent[q], spr[q, :, :, cols], v)
            ch[k, :, :, cols] = v
            return 0

        lax.fori_loop(0, 4, fill, 0)
        ch[k, :, :, zlane] += on_diag(nz[k : k + 1, :])
        outs.append(pltpu.make_async_copy(ch.at[k], ch_out.at[k], out_sem.at[k]))
        outs[-1].start()
        if k == 1:
            pg[...] = pgr[...]
            outs[0].start()
            pc[...] = pcr[...]
            for j in range(2):
                pc[j, :, :, zlane] += on_diag(sw[j : j + 1, :])
            outs[1].start()
    for cp in outs:
        cp.wait()


def on_device(cc, cw, po, a, b, sw, iw, pcov, nz):
    any_, vmem, smem = (pl.BlockSpec(memory_space=m) for m in (pl.ANY, pltpu.VMEM, pltpu.SMEM))
    v, dma = pltpu.VMEM, pltpu.SemaphoreType.DMA
    scratch = [
        v((8, 32, 1024), F32),
        v((8, 4, 2, 16, 1024), BF16),
        v((8, 4, 2, 16, 256), BF16),
        v((8, 4, 2, 16, 1024), BF16),
        v((320, 1536), BF16),
        v((8, 4, 2, 16, 128 * BLOCKS + 128), BF16),
        v((8, 4, 2, 16, 128 * BLOCKS), BF16),
        v((320, 1024), F32),
        v((4, 2, 16, 1024), F32),
        v((4, 16, 1024), F32),
        v((8, 128), F32),
        v((8, 128), F32),
        v((2, 256), F32),
        v((2, 256), F32),
        v((2, 32, 1024), BF16),
        v((2, 32, 128 * BLOCKS), BF16),
        v((4, 16, 128 * BLOCKS + 128), BF16),
        v((320, 1024), BF16),
        v((320, 1024), BF16),
        v((320, 1024), F32),
        v((256, 1024), F32),
        v((256, 1024), BF16),
        v((256, 1024), BF16),
        v((64, 1536), BF16),
        v((64, 1024), F32),
        v((4, 16, 1024), F32),
        v((2, 2, 16, 1024), F32),
        v((2, 8, 1024), F32),
        v((4, 16, 1024), F32),
        v((4, 2, 16, 1024), F32),
        v((16, 1024), F32),
        v((2, 16, 512), F32),
        pltpu.SMEM((8,), jnp.int32), pltpu.SMEM((8,), jnp.int32),
        dma((7,)), dma((1,)), dma((4,)),
        dma((3,)), dma((3,)),
        dma((4,)), dma((4,)),
        dma((4, 2)), dma((4,)),
        dma((2, 4, 4)), dma((2, 4, 4)), dma((2, 5, 4)), dma((2, 5, 4)),
        dma((7,)), dma((7,)), dma((7,)), dma((7,)), dma((4,)), dma((4,)),
        dma((4,)), dma((4,)),
        dma((4,)), dma((4, 2)),
        dma((4, 2)), dma((4, 2)), dma((4, 2)), dma((4, 2)),
        dma((3,)), dma((3,)), dma((3,)),
    ]
    pcr, pgr, spr = pl.pallas_call(
        kernel,
        out_shape=(v((2, 2, 16, 1024), F32), v((2, 8, 1024), F32), v((4, 2, 16, 1024), F32)),
        in_specs=[any_] * 7,
        out_specs=(any_, any_, any_),
        scratch_shapes=scratch,
        compiler_params=pltpu.CompilerParams(collective_id=0, has_side_effects=True),
    )(cw, po, cc, a.reshape(8, 4, 2, 16, 1024), b.reshape(8, 4, 2, 16, 256), iw, pcov)
    pc, pg, ch = pl.pallas_call(
        finish,
        out_shape=(
            jax.ShapeDtypeStruct((2, 2, 16, 1024), F32),
            jax.ShapeDtypeStruct((2, 8, 1024), F32),
            jax.ShapeDtypeStruct((8, 2, 16, 1024), F32),
        ),
        in_specs=[smem] + [vmem] * 5,
        out_specs=(any_, any_, any_),
        scratch_shapes=[
            v((2, 2, 16, 1024), F32), v((2, 8, 1024), F32), v((8, 2, 16, 1024), F32), dma((10,)),
        ],
        compiler_params=pltpu.CompilerParams(vmem_limit_bytes=8 * 2**20),
    )(po, sw, nz, pcr, pgr, spr)
    return pc.reshape(2, 32, 1024), pg, ch.reshape(8, 32, 1024)


def solution(mesh):
    rows = P("node", "tile", None)
    placed = (rows, P("node"), P("node"), P(), P(), P("node", "tile"), P("node", None), rows, P("node", "tile"))
    return jax.shard_map(
        on_device, mesh=mesh, in_specs=placed, out_specs=(rows, rows, rows), check_vma=False
    )
```

```python
import functools

import jax
import jax.numpy as jnp
from jax import lax
from jax.experimental import pallas as pl
from jax.experimental.pallas import tpu as pltpu
from jax.sharding import PartitionSpec as P

F32, BF16 = jnp.float32, jnp.bfloat16
MESH = pl.DeviceIdType.MESH


def split(v):
    high = v.astype(BF16)
    return high, (v - high.astype(F32)).astype(BF16)


def mm(a, b, dims=((1,), (0,))):
    return lax.dot_general(a, b, (dims, ((), ())), preferred_element_type=F32)


def mm2(a, b, dims=((1,), (0,))):
    m = a[0].shape[0]
    r = mm(jnp.concatenate(a, axis=0), b, dims)
    return r[:m] + r[m:]


def mm3(a, b, dims=((1,), (0,))):
    if dims[0] == (0,):
        return mm(a[0], b[0], dims) + (mm(a[0], b[1], dims) + mm(a[1], b[0], dims))
    return mm2(a, b[0], dims) + mm(a[0], b[1], dims)


def total(terms):
    while len(terms) > 1:
        terms = [
            terms[i] + terms[i + 1] if i + 1 < len(terms) else terms[i]
            for i in range(0, len(terms), 2)
        ]
    return terms[0]


def small_inverse(d):
    b = len(d)
    if b == 2:
        r = 1.0 / (d[0][0] * d[1][1] - d[0][1] * d[0][1])
        off = -d[0][1] * r
        return [[d[1][1] * r, off], [off, d[0][0] * r]]
    h = b // 2
    span = range(h)
    x = small_inverse([[d[i][j] for j in span] for i in span])
    y = [[d[i][h + j] for j in span] for i in span]
    w = [[total([x[i][k] * y[k][j] for k in span]) for j in span] for i in span]
    s = [[None] * h for _ in span]
    for i in span:
        for j in range(i, h):
            s[i][j] = s[j][i] = d[h + i][h + j] - total([y[k][i] * w[k][j] for k in span])
    q = small_inverse(s)
    wq = [[total([w[i][k] * q[k][j] for k in span]) for j in span] for i in span]
    out = [[None] * b for _ in range(b)]
    for i in span:
        for j in range(i, h):
            out[i][j] = out[j][i] = x[i][j] + total([wq[i][k] * w[j][k] for k in span])
        for j in span:
            out[i][h + j] = out[h + j][i] = -wq[i][j]
            out[h + i][h + j] = q[i][j]
    return out


def sweep(a, trips, beside=None, b=4, unroll=32):
    n = a.shape[0]
    lane = lax.broadcasted_iota(jnp.int32, (1, n), 1)
    lanes = lax.broadcasted_iota(jnp.int32, (n, n), 1)
    sub = lax.broadcasted_iota(jnp.int32, (n, 1), 0)

    def body(trip, a):
        if beside is not None:
            beside(trip)
        for low in range(0, unroll, b):
            ks = range(low, low + b)
            d = [[jnp.broadcast_to(a[i : i + 1, j : j + 1], (1, n)) for j in ks] for i in ks]
            inv = small_inverse(d)
            rows = [a[j : j + 1, :] for j in ks]
            in_rows = (sub >= low) & (sub < low + b)
            cols = [jnp.where(sub == k, -1.0, jnp.where(in_rows, 0.0, a[:, k : k + 1])) for k in ks]
            new = []
            for i in range(b):
                t = total([inv[i][j] * rows[j] for j in range(b)])
                for j in range(b):
                    t = jnp.where(lane == low + j, inv[i][j], t)
                new.append(t)
            a = jnp.where(((lanes >= low) & (lanes < low + b)) | in_rows, 0.0, a)
            for i in range(b):
                a = a - cols[i] * new[i]
        a = jnp.concatenate([a[unroll:], a[:unroll]], axis=0)
        return pltpu.roll(a, n - unroll, 1)

    return lax.fori_loop(0, trips, body, a)


ORDER = (0, 1, 3, 2)
HOPS = ((4, 3, 3, 4), (3, 4, 4, 3))
NEAR = (1, -1, 2, -2, 3, -3)
BLOCKS = 5


def place():
    n, t = lax.axis_index("node"), lax.axis_index("tile")
    return lax.rem(n, 2), n // 2, t // 4, lax.rem(t, 4)


def kernel(
    cw_in, po_in, cc, a_in, b_in, iw_in, pcov_in,
    pcr_out, pgr_out, spr_out,
    ccv, a5, b5, at5, lt, e5, p5, acc, mine, theirs, wt, wr, iw, iwr, pcov, pk, eb,
    bh, bl, cpl, gv, gh, gl, cl2, mom, pcv, pcr, pgr, spv, spr, cost_via, spread_via, cw, po,
    load_sem, loc_sem, out_sem, sa_s, sa_r, sb_s, sb_r, pa_s, pa_r,
    er_s, er_r, ef_s, ef_r, pr_s, pr_r, pf_s, pf_r, far_s, far_r,
    gs_s, gs_r, cs_s, cs_r, ss_s, ss_r, sf_s, sf_r, via_s, via_r, on_s,
):
    c, y, z, x = place()
    oc = 1 - c
    own, jq = x // 2, lax.rem(x, 2)

    def dev(core, zz, xx):
        return (2 * y + core, 4 * zz + xx)

    def xs(dx):
        return lax.rem(x + dx + 4, 4)

    def zs(dz):
        return lax.rem(z + dz + 8, 8)

    def remote(src, dst, ssem, rsem, where):
        return pltpu.make_async_remote_copy(
            src_ref=src, dst_ref=dst, send_sem=ssem, recv_sem=rsem,
            device_id=where, device_id_type=MESH,
        )

    def lanes(block):
        return pl.ds(pl.multiple_of(lax.rem(block, 8) * 128, 128), 128)

    barrier = pltpu.get_barrier_semaphore()
    for dx in range(4):
        for core in ((oc,) if dx == 0 else (c, oc)):
            pl.semaphore_signal(barrier, inc=1, device_id=dev(core, z, xs(dx)), device_id_type=MESH)
    for dz in (1, -1, 2, -2):
        pl.semaphore_signal(barrier, inc=1, device_id=dev(c, zs(dz), x), device_id_type=MESH)

    loads = [
        pltpu.make_async_copy(cc, ccv, load_sem.at[0]),
        pltpu.make_async_copy(b_in, b5, load_sem.at[1]),
        pltpu.make_async_copy(a_in, a5, load_sem.at[2]),
        pltpu.make_async_copy(iw_in, iw, load_sem.at[3]),
        pltpu.make_async_copy(pcov_in, pcov, load_sem.at[4]),
        pltpu.make_async_copy(cw_in, cw, load_sem.at[5]),
        pltpu.make_async_copy(po_in, po, load_sem.at[6]),
    ]
    for i in (5, 6, 0, 1, 2, 3, 4):
        loads[i].start()
    loads[5].wait()
    loads[6].wait()

    first = 4 * y
    coef = [
        [jnp.where(po[k] == first + q, cw[k].astype(F32), 0.0) for q in range(4)]
        for k in range(8)
    ]
    sub8 = lax.broadcasted_iota(jnp.int32, (8, 128), 0)
    tile = jnp.zeros((8, 128), F32)
    for q in range(4):
        s = total([coef[k][q] for k in range(8)])
        tile = jnp.where(sub8 == q, s, tile)
    wt[...] = tile

    loads[0].wait()

    def weigh(i, _):
        cols = pl.ds(pl.multiple_of(i * 256, 256), 256)
        for h in range(2):
            sums = [None] * 4
            for k in range(8):
                v = ccv[k, 16 * h : 16 * h + 16, cols]
                for q in range(4):
                    term = coef[k][q] * v
                    sums[q] = term if k == 0 else sums[q] + term
            for q in range(4):
                mine[q, h, :, cols] = sums[q]
        return 0

    lax.fori_loop(0, 4, weigh, 0)

    loads[3].wait()
    pl.semaphore_wait(barrier, 11)

    pair = dev(oc, z, x)
    swap = [
        remote(mine.at[:, oc], theirs, sa_s.at[0], sa_r.at[0], pair),
        remote(wt, wr, sa_s.at[1], sa_r.at[1], pair),
        remote(iw, iwr, sa_s.at[2], sa_r.at[2], pair),
    ]
    for cp in swap:
        cp.start()

    for cp in swap:
        cp.wait_recv()
    wsum = wt[...] + wr[...]
    for q in range(4):
        w = wsum[q : q + 1, 0:1]
        for p in range(BLOCKS):
            e = (mine[q, c, :, lanes(z + p)] + theirs[q, :, lanes(z + p)]) / w
            high = e.astype(BF16)
            eb[q, :, 128 * p : 128 * p + 128] = high
            if p == 0:
                eb[q, :, 128 * BLOCKS :] = (e - high.astype(F32)).astype(BF16)

    spread_e = [
        remote(eb.at[xs(dx)], e5.at[z, x, c], sb_s.at[dx], sb_r.at[dx], dev(c, z, xs(dx)))
        for dx in (2, 1, 3)
    ]
    for cp in spread_e:
        cp.start()
    e5[z, x, c] = eb[x]

    def cov_copy(dx, other):
        q = xs(dx)
        core = oc if other else c
        return remote(
            pk.at[lax.rem(q, 2), pl.ds(pl.multiple_of(16 * core, 16), 16)],
            p5.at[z, x, core], pa_s.at[dx, int(other)], pa_r.at[dx], dev(core, z, q),
        )

    def cov_local():
        return pltpu.make_async_copy(
            pk.at[jq, pl.ds(pl.multiple_of(16 * c, 16), 16)], p5.at[z, x, c], loc_sem.at[0]
        )

    def cov_start():
        for dx in (2, 1, 3, 0):
            @pl.when(xs(dx) // 2 == c)
            def _(dx=dx):
                cov_copy(dx, True).start()
                (cov_copy(dx, False) if dx else cov_local()).start()

    def cov_wait():
        for dx in (2, 1, 3):
            remote(pk.at[0, 0:16], p5.at[z, xs(-dx), c], pa_s.at[dx, 0], pa_r.at[dx], pair).wait_recv()

        @pl.when(own == c)
        def _():
            cov_local().wait()

        @pl.when(own != c)
        def _():
            remote(pk.at[0, 0:16], p5.at[z, x, c], pa_s.at[0, 0], pa_r.at[0], pair).wait_recv()

    def ring(buf, ssem, rsem, d, s, h, got):
        sign = 1 - 2 * d
        part = buf.at[zs(-sign * (s if got else s - 1)), xs(-h), c]
        return remote(part, part, ssem.at[d, s - 1, h], rsem.at[d, s - 1, h], dev(c, zs(sign), x))

    def hand(buf, fs, fr, d, s, h, core):
        sign = 1 - 2 * d
        part = buf.at[zs(-sign * s), xs(-h), core]
        return remote(part, part, fs.at[d, s, h], fr.at[d, s, h], pair)

    def ring_start(buf, ssem, rsem, fs, fr, h):
        for d in (0, 1):
            ring(buf, ssem, rsem, d, 1, h, False).start()
        hand(buf, fs, fr, 0, 0, h, c).start()

    def ring_step(buf, ssem, rsem, fs, fr, s, pieces=ORDER):
        for h in pieces:
            for d in (0, 1):
                if s <= HOPS[d][h]:
                    ring(buf, ssem, rsem, d, s, h, True).wait_recv()
                    if s < HOPS[d][h]:
                        ring(buf, ssem, rsem, d, s + 1, h, False).start()
                    hand(buf, fs, fr, d, s, h, c).start()

    def hand_wait(buf, fs, fr, s):
        for h in ORDER:
            for d in (0,) if s == 0 else (0, 1):
                if s <= HOPS[d][h]:
                    hand(buf, fs, fr, d, s, h, oc).wait_recv()

    def drain(buf, ssem, rsem, fs, fr):
        for h in ORDER:
            hand(buf, fs, fr, 0, 0, h, c).wait_send()
            for d in range(2):
                for s in range(1, HOPS[d][h] + 1):
                    ring(buf, ssem, rsem, d, s, h, False).wait_send()
                    hand(buf, fs, fr, d, s, h, c).wait_send()

    e_ring = (e5, er_s, er_r, ef_s, ef_r)

    def cov_send(dz):
        if abs(dz) == 3:
            held, hop = zs(-2 * dz // 3), dz // 3
        else:
            held, hop = z, dz
        part = p5.at[held, :, c]
        return remote(part, part, pr_s.at[dz + 3], pr_r.at[dz + 3], dev(c, zs(hop), x))

    def cov_got(dz):
        part = p5.at[zs(-dz), :, c]
        return remote(part, part, pr_s.at[dz + 3], pr_r.at[dz + 3], pair)

    def cov_hand(dz, core):
        part = p5.at[zs(-dz), :, core]
        return remote(part, part, pf_s.at[dz + 3], pf_r.at[dz + 3], pair)

    def cov_onward(d, got=False):
        sign = 1 - 2 * d
        part = p5.at[zs(4 if got else -3 * sign), pl.ds(2 * d, 2), c]
        return remote(part, part, far_s.at[d], far_r.at[d], dev(c, zs(sign), x))

    def cov_far_hand(d, core):
        part = p5.at[zs(4), pl.ds(2 * d, 2), core]
        return remote(part, part, far_s.at[2 + d], far_r.at[2 + d], pair)

    def cov_take(dz):
        cov_got(dz).wait_recv()
        cov_hand(dz, c).start()


    def chunk_add(buf, zc, left2, out):
        left = left2[:, lanes(zc)]
        chunk = buf[zc].reshape(128, buf.shape[-1])
        for p in range(BLOCKS):
            v = mm(left, chunk[:, 128 * p : 128 * p + 128])
            if p == 0 and buf.shape[-1] > 128 * BLOCKS:
                v = v + mm(left, chunk[:, 128 * BLOCKS :])
            out[:, lanes(zc + p)] += v
        turned = left2[:, pl.ds(pl.multiple_of(128 * zc + 128, 128), 384)]
        out[:, lanes(zc)] += mm(turned, chunk[:, 128:512], ((1,), (1,)))

    ring_start(*e_ring, 0)
    loads[1].wait()
    lt[0:256, 0:1024] = b5[...].reshape(1024, 256).T
    loads[2].wait()

    def turn(i, _):
        block = a5[pl.ds(i, 1)].reshape(128, 1024)
        at5[:, :, :, :, pl.ds(pl.multiple_of(i * 128, 128), 128)] = block.T.reshape(8, 4, 2, 16, 128)
        return 0

    lax.fori_loop(0, 8, turn, 0)
    lt[256:320, 0:1024] = at5[z, :, c].reshape(64, 1024)
    lt[:, 1024:1536] = lt[:, 0:512]
    loads[4].wait()
    for p in range(BLOCKS):
        pk[:, :, 128 * p : 128 * p + 128] = pcov[:, :, lanes(z + p)]
    acc[...] = jnp.zeros_like(acc)
    for dx in ORDER[1:]:
        remote(eb.at[xs(dx)], e5.at[z, xs(-dx), c], sb_s.at[dx], sb_r.at[dx], dev(c, z, xs(dx))).wait_recv()
        ring_start(*e_ring, dx)
    cov_start()
    ring_step(*e_ring, 1)
    hand_wait(e5, ef_s, ef_r, 0)
    chunk_add(e5, z, lt, acc)
    ring_step(*e_ring, 2)
    hand_wait(e5, ef_s, ef_r, 1)
    chunk_add(e5, zs(1), lt, acc)
    ring_step(*e_ring, 3)
    chunk_add(e5, zs(-1), lt, acc)
    hand_wait(e5, ef_s, ef_r, 2)
    chunk_add(e5, zs(2), lt, acc)
    chunk_add(e5, zs(-2), lt, acc)
    ring_step(*e_ring, 4)
    cov_wait()
    cov_hand(0, c).start()
    for dz in NEAR[:4]:
        cov_send(dz).start()
    hand_wait(e5, ef_s, ef_r, 3)
    chunk_add(e5, zs(3), lt, acc)
    chunk_add(e5, zs(-3), lt, acc)
    hand_wait(e5, ef_s, ef_r, 4)
    chunk_add(e5, zs(4), lt, acc)

    hi, lo = split(acc[...])
    bh[...] = hi
    bl[...] = lo
    bfull = b5[...].reshape(1024, 256)
    small = mm(bh[...], bfull) + mm(bl[...], bfull)
    weights = jnp.where(own == c, iw[pl.ds(jq, 1), :], iwr[pl.ds(jq, 1), :])
    r256 = lax.broadcasted_iota(jnp.int32, (256, 256), 0)
    c256 = lax.broadcasted_iota(jnp.int32, (256, 256), 1)
    curv = small[0:256] + jnp.where(r256 == c256, weights, 0.0)
    cpl_own = split(small[256:320])

    def times_a(trip):
        for part in range(2):
            cols = pl.ds(pl.multiple_of(trip * 512 + part * 256, 256), 256)
            right = a5[:, :, :, :, cols].reshape(1024, 256)
            cpl[:, cols] = mm(bh[...], right) + mm(bl[...], right)

    s11, s12, s22 = curv[:128, :128], curv[:128, 128:], curv[128:, 128:]
    inv = sweep(s11, 2, times_a)
    inv = sweep(inv, 2)
    for dz in NEAR[:4]:
        cov_take(dz)
        if abs(dz) == 2:
            cov_send(3 * dz // 2).start()
    inv_s, s12_s = split(inv), split(s12)
    w = mm3(inv_s, s12_s)
    w_s = split(w)
    inv2 = sweep(s22 - mm3(s12_s, w_s, ((0,), (0,))), 2)
    for d in range(2):
        cov_take(3 - 6 * d)
        cov_onward(d).start()
    inv2 = sweep(inv2, 2)
    wq = mm3(w_s, split(inv2))
    inv1 = inv + mm3(split(wq), w_s, ((1,), (1,)))
    full_s = split(
        jnp.concatenate(
            [jnp.concatenate([inv1, -wq], axis=1), jnp.concatenate([-wq.T, inv2], axis=1)], axis=0
        )
    )

    for i in range(4):
        cols = slice(256 * i, 256 * i + 256)
        g = mm3(full_s, split(cpl[0:256, cols]))
        gv[:, cols] = g
        gh[:, cols], gl[:, cols] = split(g)

    for d in range(2):
        cov_onward(d, True).wait_recv()
        cov_far_hand(d, c).start()

    def gain_copy(dx):
        xx = xs(dx)
        rows = pl.ds(pl.multiple_of(32 * z + 8 * xx, 8), 8)
        return remote(gv.at[rows], pgr.at[jq], gs_s.at[dx], gs_r.at[dx], dev(c, z, xx))

    @pl.when(own == c)
    def _():
        for dx in (2, 1, 3):
            gain_copy(dx).start()
        pgr[jq] = gv[pl.ds(pl.multiple_of(32 * z + 8 * x, 8), 8), :]

    for i in range(4):
        cols = slice(256 * i, 256 * i + 256)
        v = cpl[256:320, cols] - mm3(cpl_own, (gh[:, cols], gl[:, cols]))
        pcv[:, :, cols] = v.reshape(4, 16, 256)

    def cost_copy(dx):
        return remote(pcv.at[xs(dx)], pcr.at[jq, c], cs_s.at[dx], cs_r.at[dx, c], dev(own, z, xs(dx)))

    way = 1 - 2 * c
    source = xs(-way)

    def cost_near():
        return remote(pcv.at[xs(2)], cost_via, via_s.at[0], via_r.at[0], dev(c, z, xs(way)))

    def cost_onward():
        return remote(
            cost_via, pcr.at[lax.rem(source, 2), c], on_s.at[0], cs_r.at[2, c], dev(source // 2, z, xs(way))
        )

    cost_near().start()
    for dx in (1, 3):
        cost_copy(dx).start()

    @pl.when(own == c)
    def _():
        pcr[jq, c] = pcv[x]

    @pl.when(own != c)
    def _():
        cost_copy(0).start()

    a_rows = a5[z, :, c].reshape(64, 1024).astype(F32)
    b_rows = b5[z, :, c].reshape(64, 256)
    closed = (a_rows - (mm(b_rows, gh[...]) + mm(b_rows, gl[...]))).astype(BF16)
    cl2[:, 0:1024] = closed
    cl2[:, 1024:1536] = closed[:, 0:512]
    for dz in (0,) + NEAR:
        cov_hand(dz, oc).wait_recv()
    for d in range(2):
        cov_far_hand(d, oc).wait_recv()
    nt = ((1,), (1,))
    for q in range(8):
        low = (q - BLOCKS + 1) % 8
        right = jnp.concatenate(
            [
                p5[(low + i) % 8, :, :, :, 128 * (BLOCKS - 1 - i) : 128 * (BLOCKS - i)].reshape(128, 128)
                for i in range(BLOCKS)
            ],
            axis=0,
        )
        mom[:, 128 * q : 128 * q + 128] = mm(cl2[:, 128 * low : 128 * (low + BLOCKS)], right) + mm(
            cl2[:, 128 * (q + 1) : 128 * (q + 4)], p5[q, :, :, :, 128:512].reshape(128, 384), nt
        )
    moment_s = split(mom[...])
    inner_s = split(mm3(moment_s, (gh[...], gl[...]), nt))

    cost_near().wait_recv()
    cost_onward().start()

    def spread_copy(dx, half):
        cols = pl.ds(512 * half, 512)
        return remote(
            spv.at[xs(dx), :, cols], spr.at[x, c, :, cols], ss_s.at[dx, half], ss_r.at[dx, half], dev(c, z, xs(dx))
        )

    def spread_got(dx, half):
        cols = pl.ds(512 * half, 512)
        return remote(
            spv.at[xs(dx), :, cols], spr.at[xs(-dx), c, :, cols], ss_s.at[dx, half], ss_r.at[dx, half], dev(c, z, xs(dx))
        )

    def spread_hand(dx, half, core):
        part = spr.at[xs(-dx), core, :, pl.ds(512 * half, 512)]
        return remote(part, part, sf_s.at[dx, half], sf_r.at[dx, half], pair)

    def spread_near(half):
        return remote(
            spv.at[xs(2), :, pl.ds(512 * half, 512)], spread_via.at[half],
            via_s.at[1 + half], via_r.at[1 + half], dev(c, z, xs(way)),
        )

    def spread_onward(half):
        return remote(
            spread_via.at[half], spr.at[source, c, :, pl.ds(512 * half, 512)],
            on_s.at[1 + half], ss_r.at[2, half], dev(c, z, xs(way)),
        )

    for half in range(2):
        for i in range(2):
            cols = slice(512 * half + 256 * i, 512 * half + 256 * i + 256)
            v = mm2(moment_s, at5[:, :, :, :, cols].reshape(1024, 256)) - mm2(inner_s, lt[0:256, cols])
            spv[:, :, cols] = v.reshape(4, 16, 256)

        spread_near(half).start()
        cols = slice(512 * half, 512 * half + 512)
        spr[x, c, :, cols] = spv[x, :, cols]
        spread_hand(0, half, c).start()

    for half in range(2):
        for dx in (1, 3):
            spread_copy(dx, half).start()
    for half in range(2):
        spread_near(half).wait_recv()
        spread_onward(half).start()

    for cp in swap + spread_e:
        cp.wait_send()
    for dx in range(4):
        @pl.when(xs(dx) // 2 == c)
        def _(dx=dx):
            cov_copy(dx, True).wait_send()
            if dx:
                cov_copy(dx, False).wait_send()
    drain(*e_ring)
    cov_hand(0, c).wait_send()
    for dz in NEAR:
        cov_send(dz).wait_send()
        cov_hand(dz, c).wait_send()
    for d in range(2):
        cov_onward(d).wait_send()
        cov_far_hand(d, c).wait_send()

    for dx in (1, 2, 3):
        @pl.when(xs(-dx) // 2 == c)
        def _(dx=dx):
            remote(gv.at[0:8], pgr.at[lax.rem(xs(-dx), 2)], gs_s.at[dx], gs_r.at[dx], pair).wait_recv()
            for core in range(2):
                remote(pcv.at[0], pcr.at[lax.rem(xs(-dx), 2), core], cs_s.at[dx], cs_r.at[dx, core], pair).wait_recv()

    @pl.when(own == c)
    def _():
        remote(pcv.at[0], pcr.at[jq, oc], cs_s.at[0], cs_r.at[0, oc], pair).wait_recv()

    out_pg = pltpu.make_async_copy(pgr, pgr_out, out_sem.at[0])
    out_pg.start()
    out_pc = pltpu.make_async_copy(pcr, pcr_out, out_sem.at[1])
    out_pc.start()

    for half in range(2):
        for dx in (1, 3, 2):
            spread_got(dx, half).wait_recv()
            spread_hand(dx, half, c).start()
    out_own = pltpu.make_async_copy(spr.at[:, c], spr_out.at[:, c], out_sem.at[2])
    out_own.start()
    for half in range(2):
        for dx in range(4):
            spread_hand(dx, half, oc).wait_recv()
    out_pair = pltpu.make_async_copy(spr.at[:, oc], spr_out.at[:, oc], out_sem.at[3])
    out_pair.start()

    @pl.when(own == c)
    def _():
        for dx in (2, 1, 3):
            gain_copy(dx).wait_send()

    @pl.when(own != c)
    def _():
        cost_copy(0).wait_send()

    cost_near().wait_send()
    cost_onward().wait_send()
    for half in range(2):
        spread_near(half).wait_send()
        spread_onward(half).wait_send()
    for dx in (1, 3):
        cost_copy(dx).wait_send()
        for half in range(2):
            spread_copy(dx, half).wait_send()
    for half in range(2):
        for dx in range(4):
            spread_hand(dx, half, c).wait_send()
    out_pg.wait()
    out_pc.wait()
    out_own.wait()
    out_pair.wait()


def finish(po, sw, nz, pcr, pgr, spr, pc_out, pg_out, ch_out, pc, pg, ch, out_sem):
    outs = [
        pltpu.make_async_copy(pg, pg_out, out_sem.at[8]),
        pltpu.make_async_copy(pc, pc_out, out_sem.at[9]),
    ]
    c, y, z, x = place()
    zlane = pl.ds(pl.multiple_of(z * 128, 128), 128)
    diag = lax.broadcasted_iota(jnp.int32, (32, 128), 1) == (
        32 * x + lax.broadcasted_iota(jnp.int32, (32, 128), 0)
    )
    pick = lax.broadcasted_iota(jnp.int32, (32, 32), 1) == lax.broadcasted_iota(jnp.int32, (32, 32), 0)

    def on_diag(row):
        column = jnp.sum(jnp.where(pick, row, 0.0), axis=1, keepdims=True)
        return jnp.where(diag, column, 0.0).reshape(2, 16, 128)

    for k in range(8):
        parent = [po[k] == 4 * y + q for q in range(4)]

        def fill(i, _):
            cols = pl.ds(pl.multiple_of(i * 256, 256), 256)
            v = spr[0, :, :, cols]
            for q in range(1, 4):
                v = jnp.where(parent[q], spr[q, :, :, cols], v)
            ch[k, :, :, cols] = v
            return 0

        lax.fori_loop(0, 4, fill, 0)
        ch[k, :, :, zlane] += on_diag(nz[k : k + 1, :])
        outs.append(pltpu.make_async_copy(ch.at[k], ch_out.at[k], out_sem.at[k]))
        outs[-1].start()
        if k == 1:
            pg[...] = pgr[...]
            outs[0].start()
            pc[...] = pcr[...]
            for j in range(2):
                pc[j, :, :, zlane] += on_diag(sw[j : j + 1, :])
            outs[1].start()
    for cp in outs:
        cp.wait()


def on_device(cc, cw, po, a, b, sw, iw, pcov, nz):
    any_, vmem, smem = (pl.BlockSpec(memory_space=m) for m in (pl.ANY, pltpu.VMEM, pltpu.SMEM))
    v, dma = pltpu.VMEM, pltpu.SemaphoreType.DMA
    scratch = [
        v((8, 32, 1024), F32),
        v((8, 4, 2, 16, 1024), BF16),
        v((8, 4, 2, 16, 256), BF16),
        v((8, 4, 2, 16, 1024), BF16),
        v((320, 1536), BF16),
        v((8, 4, 2, 16, 128 * BLOCKS + 128), BF16),
        v((8, 4, 2, 16, 128 * BLOCKS), BF16),
        v((320, 1024), F32),
        v((4, 2, 16, 1024), F32),
        v((4, 16, 1024), F32),
        v((8, 128), F32),
        v((8, 128), F32),
        v((2, 256), F32),
        v((2, 256), F32),
        v((2, 32, 1024), BF16),
        v((2, 32, 128 * BLOCKS), BF16),
        v((4, 16, 128 * BLOCKS + 128), BF16),
        v((320, 1024), BF16),
        v((320, 1024), BF16),
        v((320, 1024), F32),
        v((256, 1024), F32),
        v((256, 1024), BF16),
        v((256, 1024), BF16),
        v((64, 1536), BF16),
        v((64, 1024), F32),
        v((4, 16, 1024), F32),
        v((2, 2, 16, 1024), F32),
        v((2, 8, 1024), F32),
        v((4, 16, 1024), F32),
        v((4, 2, 16, 1024), F32),
        v((16, 1024), F32),
        v((2, 16, 512), F32),
        pltpu.SMEM((8,), jnp.int32), pltpu.SMEM((8,), jnp.int32),
        dma((7,)), dma((1,)), dma((4,)),
        dma((3,)), dma((3,)),
        dma((4,)), dma((4,)),
        dma((4, 2)), dma((4,)),
        dma((2, 4, 4)), dma((2, 4, 4)), dma((2, 5, 4)), dma((2, 5, 4)),
        dma((7,)), dma((7,)), dma((7,)), dma((7,)), dma((4,)), dma((4,)),
        dma((4,)), dma((4,)),
        dma((4,)), dma((4, 2)),
        dma((4, 2)), dma((4, 2)), dma((4, 2)), dma((4, 2)),
        dma((3,)), dma((3,)), dma((3,)),
    ]
    pcr, pgr, spr = pl.pallas_call(
        kernel,
        out_shape=(v((2, 2, 16, 1024), F32), v((2, 8, 1024), F32), v((4, 2, 16, 1024), F32)),
        in_specs=[any_] * 7,
        out_specs=(any_, any_, any_),
        scratch_shapes=scratch,
        compiler_params=pltpu.CompilerParams(collective_id=0, has_side_effects=True),
    )(cw, po, cc, a.reshape(8, 4, 2, 16, 1024), b.reshape(8, 4, 2, 16, 256), iw, pcov)
    pc, pg, ch = pl.pallas_call(
        finish,
        out_shape=(
            jax.ShapeDtypeStruct((2, 2, 16, 1024), F32),
            jax.ShapeDtypeStruct((2, 8, 1024), F32),
            jax.ShapeDtypeStruct((8, 2, 16, 1024), F32),
        ),
        in_specs=[smem] + [vmem] * 5,
        out_specs=(any_, any_, any_),
        scratch_shapes=[
            v((2, 2, 16, 1024), F32), v((2, 8, 1024), F32), v((8, 2, 16, 1024), F32), dma((10,)),
        ],
        compiler_params=pltpu.CompilerParams(vmem_limit_bytes=8 * 2**20),
    )(po, sw, nz, pcr, pgr, spr)
    return pc.reshape(2, 32, 1024), pg, ch.reshape(8, 32, 1024)


def solution(mesh):
    rows = P("node", "tile", None)
    placed = (rows, P("node"), P("node"), P(), P(), P("node", "tile"), P("node", None), rows, P("node", "tile"))
    return jax.shard_map(
        on_device, mesh=mesh, in_specs=placed, out_specs=(rows, rows, rows), check_vma=False
    )
```

```python
import functools

import jax
import jax.numpy as jnp
from jax import lax
from jax.experimental import pallas as pl
from jax.experimental.pallas import tpu as pltpu
from jax.sharding import PartitionSpec as P

F32, BF16 = jnp.float32, jnp.bfloat16
MESH = pl.DeviceIdType.MESH


def split(v):
    high = v.astype(BF16)
    return high, (v - high.astype(F32)).astype(BF16)


def mm(a, b, dims=((1,), (0,))):
    return lax.dot_general(a, b, (dims, ((), ())), preferred_element_type=F32)


def mm2(a, b, dims=((1,), (0,))):
    m = a[0].shape[0]
    r = mm(jnp.concatenate(a, axis=0), b, dims)
    return r[:m] + r[m:]


def mm3(a, b, dims=((1,), (0,))):
    if dims[0] == (0,):
        return mm(a[0], b[0], dims) + (mm(a[0], b[1], dims) + mm(a[1], b[0], dims))
    return mm2(a, b[0], dims) + mm(a[0], b[1], dims)


def total(terms):
    while len(terms) > 1:
        terms = [
            terms[i] + terms[i + 1] if i + 1 < len(terms) else terms[i]
            for i in range(0, len(terms), 2)
        ]
    return terms[0]


def small_inverse(d):
    b = len(d)
    if b == 2:
        r = 1.0 / (d[0][0] * d[1][1] - d[0][1] * d[0][1])
        off = -d[0][1] * r
        return [[d[1][1] * r, off], [off, d[0][0] * r]]
    h = b // 2
    span = range(h)
    x = small_inverse([[d[i][j] for j in span] for i in span])
    y = [[d[i][h + j] for j in span] for i in span]
    w = [[total([x[i][k] * y[k][j] for k in span]) for j in span] for i in span]
    s = [[None] * h for _ in span]
    for i in span:
        for j in range(i, h):
            s[i][j] = s[j][i] = d[h + i][h + j] - total([y[k][i] * w[k][j] for k in span])
    q = small_inverse(s)
    wq = [[total([w[i][k] * q[k][j] for k in span]) for j in span] for i in span]
    out = [[None] * b for _ in range(b)]
    for i in span:
        for j in range(i, h):
            out[i][j] = out[j][i] = x[i][j] + total([wq[i][k] * w[j][k] for k in span])
        for j in span:
            out[i][h + j] = out[h + j][i] = -wq[i][j]
            out[h + i][h + j] = q[i][j]
    return out


def sweep(a, trips, beside=None, b=4, unroll=32):
    n = a.shape[0]
    lane = lax.broadcasted_iota(jnp.int32, (1, n), 1)
    lanes = lax.broadcasted_iota(jnp.int32, (n, n), 1)
    sub = lax.broadcasted_iota(jnp.int32, (n, 1), 0)

    def body(trip, a):
        if beside is not None:
            beside(trip)
        for low in range(0, unroll, b):
            ks = range(low, low + b)
            d = [[jnp.broadcast_to(a[i : i + 1, j : j + 1], (1, n)) for j in ks] for i in ks]
            inv = small_inverse(d)
            rows = [a[j : j + 1, :] for j in ks]
            in_rows = (sub >= low) & (sub < low + b)
            cols = [jnp.where(sub == k, -1.0, jnp.where(in_rows, 0.0, a[:, k : k + 1])) for k in ks]
            new = []
            for i in range(b):
                t = total([inv[i][j] * rows[j] for j in range(b)])
                for j in range(b):
                    t = jnp.where(lane == low + j, inv[i][j], t)
                new.append(t)
            a = jnp.where(((lanes >= low) & (lanes < low + b)) | in_rows, 0.0, a)
            for i in range(b):
                a = a - cols[i] * new[i]
        a = jnp.concatenate([a[unroll:], a[:unroll]], axis=0)
        return pltpu.roll(a, n - unroll, 1)

    return lax.fori_loop(0, trips, body, a)


ORDER = (0, 1, 3, 2)
HOPS = ((4, 3, 3, 4), (3, 4, 4, 3))
NEAR = (3, -3, 2, -2, 1, -1)
BLOCKS = 5


def place():
    n, t = lax.axis_index("node"), lax.axis_index("tile")
    return lax.rem(n, 2), n // 2, t // 4, lax.rem(t, 4)


def kernel(
    cw_in, po_in, cc, a_in, b_in, iw_in, pcov_in,
    pcr_out, pgr_out, spr_out,
    ccv, a5, b5, at5, lt, e5, p5, acc, mine, theirs, wt, wr, iw, iwr, pcov, pk, eb,
    bh, bl, cpl, gv, gh, gl, cl2, mom, pcv, pcr, pgr, spv, spr, cost_via, spread_via, cw, po,
    load_sem, loc_sem, out_sem, sa_s, sa_r, sb_s, sb_r, pa_s, pa_r,
    er_s, er_r, ef_s, ef_r, pr_s, pr_r, pf_s, pf_r, far_s, far_r,
    gs_s, gs_r, cs_s, cs_r, ss_s, ss_r, sf_s, sf_r, via_s, via_r, on_s,
):
    c, y, z, x = place()
    oc = 1 - c
    own, jq = x // 2, lax.rem(x, 2)

    def dev(core, zz, xx):
        return (2 * y + core, 4 * zz + xx)

    def xs(dx):
        return lax.rem(x + dx + 4, 4)

    def zs(dz):
        return lax.rem(z + dz + 8, 8)

    def remote(src, dst, ssem, rsem, where):
        return pltpu.make_async_remote_copy(
            src_ref=src, dst_ref=dst, send_sem=ssem, recv_sem=rsem,
            device_id=where, device_id_type=MESH,
        )

    def lanes(block):
        return pl.ds(pl.multiple_of(lax.rem(block, 8) * 128, 128), 128)

    barrier = pltpu.get_barrier_semaphore()
    for dx in range(4):
        for core in ((oc,) if dx == 0 else (c, oc)):
            pl.semaphore_signal(barrier, inc=1, device_id=dev(core, z, xs(dx)), device_id_type=MESH)
    for dz in range(1, 8):
        pl.semaphore_signal(barrier, inc=1, device_id=dev(c, zs(dz), x), device_id_type=MESH)

    loads = [
        pltpu.make_async_copy(cc, ccv, load_sem.at[0]),
        pltpu.make_async_copy(b_in, b5, load_sem.at[1]),
        pltpu.make_async_copy(a_in, a5, load_sem.at[2]),
        pltpu.make_async_copy(iw_in, iw, load_sem.at[3]),
        pltpu.make_async_copy(pcov_in, pcov, load_sem.at[4]),
        pltpu.make_async_copy(cw_in, cw, load_sem.at[5]),
        pltpu.make_async_copy(po_in, po, load_sem.at[6]),
    ]
    for i in (5, 6, 0, 1, 2, 3, 4):
        loads[i].start()
    loads[5].wait()
    loads[6].wait()

    first = 4 * y
    coef = [
        [jnp.where(po[k] == first + q, cw[k].astype(F32), 0.0) for q in range(4)]
        for k in range(8)
    ]
    sub8 = lax.broadcasted_iota(jnp.int32, (8, 128), 0)
    tile = jnp.zeros((8, 128), F32)
    for q in range(4):
        s = total([coef[k][q] for k in range(8)])
        tile = jnp.where(sub8 == q, s, tile)
    wt[...] = tile

    loads[0].wait()

    def weigh(i, _):
        cols = pl.ds(pl.multiple_of(i * 256, 256), 256)
        for h in range(2):
            sums = [None] * 4
            for k in range(8):
                v = ccv[k, 16 * h : 16 * h + 16, cols]
                for q in range(4):
                    term = coef[k][q] * v
                    sums[q] = term if k == 0 else sums[q] + term
            for q in range(4):
                mine[q, h, :, cols] = sums[q]
        return 0

    lax.fori_loop(0, 4, weigh, 0)

    loads[3].wait()
    pl.semaphore_wait(barrier, 14)

    pair = dev(oc, z, x)
    swap = [
        remote(mine.at[:, oc], theirs, sa_s.at[0], sa_r.at[0], pair),
        remote(wt, wr, sa_s.at[1], sa_r.at[1], pair),
        remote(iw, iwr, sa_s.at[2], sa_r.at[2], pair),
    ]
    for cp in swap:
        cp.start()

    for cp in swap:
        cp.wait_recv()
    wsum = wt[...] + wr[...]
    for q in range(4):
        w = wsum[q : q + 1, 0:1]
        for p in range(BLOCKS):
            e = (mine[q, c, :, lanes(z + p)] + theirs[q, :, lanes(z + p)]) / w
            high = e.astype(BF16)
            eb[q, :, 128 * p : 128 * p + 128] = high
            if p == 0:
                eb[q, :, 128 * BLOCKS :] = (e - high.astype(F32)).astype(BF16)

    spread_e = [
        remote(eb.at[xs(dx)], e5.at[z, x, c], sb_s.at[dx], sb_r.at[dx], dev(c, z, xs(dx)))
        for dx in (2, 1, 3)
    ]
    for cp in spread_e:
        cp.start()
    e5[z, x, c] = eb[x]

    def cov_copy(dx, other):
        q = xs(dx)
        core = oc if other else c
        return remote(
            pk.at[lax.rem(q, 2), pl.ds(pl.multiple_of(16 * core, 16), 16)],
            p5.at[z, x, core], pa_s.at[dx, int(other)], pa_r.at[dx], dev(core, z, q),
        )

    def cov_local():
        return pltpu.make_async_copy(
            pk.at[jq, pl.ds(pl.multiple_of(16 * c, 16), 16)], p5.at[z, x, c], loc_sem.at[0]
        )

    def cov_start():
        for dx in (2, 1, 3, 0):
            @pl.when(xs(dx) // 2 == c)
            def _(dx=dx):
                cov_copy(dx, True).start()
                (cov_copy(dx, False) if dx else cov_local()).start()

    def cov_wait():
        for dx in (2, 1, 3):
            remote(pk.at[0, 0:16], p5.at[z, xs(-dx), c], pa_s.at[dx, 0], pa_r.at[dx], pair).wait_recv()

        @pl.when(own == c)
        def _():
            cov_local().wait()

        @pl.when(own != c)
        def _():
            remote(pk.at[0, 0:16], p5.at[z, x, c], pa_s.at[0, 0], pa_r.at[0], pair).wait_recv()

    def ring(buf, ssem, rsem, d, s, h, got):
        sign = 1 - 2 * d
        part = buf.at[zs(-sign * (s if got else s - 1)), xs(-h), c]
        return remote(part, part, ssem.at[d, s - 1, h], rsem.at[d, s - 1, h], dev(c, zs(sign), x))

    def hand(buf, fs, fr, d, s, h, core):
        sign = 1 - 2 * d
        part = buf.at[zs(-sign * s), xs(-h), core]
        return remote(part, part, fs.at[d, s, h], fr.at[d, s, h], pair)

    def ring_start(buf, ssem, rsem, fs, fr, h):
        for d in (0, 1):
            ring(buf, ssem, rsem, d, 1, h, False).start()
        hand(buf, fs, fr, 0, 0, h, c).start()

    def ring_step(buf, ssem, rsem, fs, fr, s, pieces=ORDER):
        for h in pieces:
            for d in (0, 1):
                if s <= HOPS[d][h]:
                    ring(buf, ssem, rsem, d, s, h, True).wait_recv()
                    if s < HOPS[d][h]:
                        ring(buf, ssem, rsem, d, s + 1, h, False).start()
                    hand(buf, fs, fr, d, s, h, c).start()

    def hand_wait(buf, fs, fr, s):
        for h in ORDER:
            for d in (0,) if s == 0 else (0, 1):
                if s <= HOPS[d][h]:
                    hand(buf, fs, fr, d, s, h, oc).wait_recv()

    def drain(buf, ssem, rsem, fs, fr):
        for h in ORDER:
            hand(buf, fs, fr, 0, 0, h, c).wait_send()
            for d in range(2):
                for s in range(1, HOPS[d][h] + 1):
                    ring(buf, ssem, rsem, d, s, h, False).wait_send()
                    hand(buf, fs, fr, d, s, h, c).wait_send()

    e_ring = (e5, er_s, er_r, ef_s, ef_r)

    def cov_send(dz):
        part = p5.at[z, :, c]
        return remote(part, part, pr_s.at[dz + 3], pr_r.at[dz + 3], dev(c, zs(dz), x))

    def cov_got(dz):
        part = p5.at[zs(-dz), :, c]
        return remote(part, part, pr_s.at[dz + 3], pr_r.at[dz + 3], pair)

    def cov_hand(dz, core):
        part = p5.at[zs(-dz), :, core]
        return remote(part, part, pf_s.at[dz + 3], pf_r.at[dz + 3], pair)

    def cov_onward(d, got=False):
        sign = 1 - 2 * d
        part = p5.at[zs(4 if got else -3 * sign), pl.ds(2 * d, 2), c]
        return remote(part, part, far_s.at[d], far_r.at[d], dev(c, zs(sign), x))

    def cov_far_hand(d, core):
        part = p5.at[zs(4), pl.ds(2 * d, 2), core]
        return remote(part, part, far_s.at[2 + d], far_r.at[2 + d], pair)

    def cov_take(dz):
        cov_got(dz).wait_recv()
        cov_hand(dz, c).start()


    def chunk_add(buf, zc, left2, out):
        left = left2[:, lanes(zc)]
        chunk = buf[zc].reshape(128, buf.shape[-1])
        for p in range(BLOCKS):
            v = mm(left, chunk[:, 128 * p : 128 * p + 128])
            if p == 0 and buf.shape[-1] > 128 * BLOCKS:
                v = v + mm(left, chunk[:, 128 * BLOCKS :])
            out[:, lanes(zc + p)] += v
        turned = left2[:, pl.ds(pl.multiple_of(128 * zc + 128, 128), 384)]
        out[:, lanes(zc)] += mm(turned, chunk[:, 128:512], ((1,), (1,)))

    ring_start(*e_ring, 0)
    loads[1].wait()
    lt[0:256, 0:1024] = b5[...].reshape(1024, 256).T
    loads[2].wait()

    def turn(i, _):
        block = a5[pl.ds(i, 1)].reshape(128, 1024)
        at5[:, :, :, :, pl.ds(pl.multiple_of(i * 128, 128), 128)] = block.T.reshape(8, 4, 2, 16, 128)
        return 0

    lax.fori_loop(0, 8, turn, 0)
    lt[256:320, 0:1024] = at5[z, :, c].reshape(64, 1024)
    lt[:, 1024:1536] = lt[:, 0:512]
    loads[4].wait()
    for p in range(BLOCKS):
        pk[:, :, 128 * p : 128 * p + 128] = pcov[:, :, lanes(z + p)]
    acc[...] = jnp.zeros_like(acc)
    for dx in ORDER[1:]:
        remote(eb.at[xs(dx)], e5.at[z, xs(-dx), c], sb_s.at[dx], sb_r.at[dx], dev(c, z, xs(dx))).wait_recv()
        ring_start(*e_ring, dx)
    cov_start()
    ring_step(*e_ring, 1)
    hand_wait(e5, ef_s, ef_r, 0)
    chunk_add(e5, z, lt, acc)
    ring_step(*e_ring, 2)
    hand_wait(e5, ef_s, ef_r, 1)
    chunk_add(e5, zs(1), lt, acc)
    ring_step(*e_ring, 3)
    chunk_add(e5, zs(-1), lt, acc)
    hand_wait(e5, ef_s, ef_r, 2)
    chunk_add(e5, zs(2), lt, acc)
    chunk_add(e5, zs(-2), lt, acc)
    ring_step(*e_ring, 4)
    cov_wait()
    cov_hand(0, c).start()
    for dz in NEAR:
        cov_send(dz).start()
    hand_wait(e5, ef_s, ef_r, 3)
    chunk_add(e5, zs(3), lt, acc)
    chunk_add(e5, zs(-3), lt, acc)
    hand_wait(e5, ef_s, ef_r, 4)
    chunk_add(e5, zs(4), lt, acc)

    hi, lo = split(acc[...])
    bh[...] = hi
    bl[...] = lo
    bfull = b5[...].reshape(1024, 256)
    small = mm(bh[...], bfull) + mm(bl[...], bfull)
    weights = jnp.where(own == c, iw[pl.ds(jq, 1), :], iwr[pl.ds(jq, 1), :])
    r256 = lax.broadcasted_iota(jnp.int32, (256, 256), 0)
    c256 = lax.broadcasted_iota(jnp.int32, (256, 256), 1)
    curv = small[0:256] + jnp.where(r256 == c256, weights, 0.0)
    cpl_own = split(small[256:320])

    def times_a(trip):
        for part in range(2):
            cols = pl.ds(pl.multiple_of(trip * 512 + part * 256, 256), 256)
            right = a5[:, :, :, :, cols].reshape(1024, 256)
            cpl[:, cols] = mm(bh[...], right) + mm(bl[...], right)

    s11, s12, s22 = curv[:128, :128], curv[:128, 128:], curv[128:, 128:]
    inv = sweep(s11, 2, times_a)
    inv = sweep(inv, 2)
    inv_s, s12_s = split(inv), split(s12)
    w = mm3(inv_s, s12_s)
    w_s = split(w)
    inv2 = sweep(s22 - mm3(s12_s, w_s, ((0,), (0,))), 2)
    for d in range(2):
        cov_take(3 - 6 * d)
        cov_onward(d).start()
    inv2 = sweep(inv2, 2)
    for dz in NEAR[2:]:
        cov_take(dz)
    wq = mm3(w_s, split(inv2))
    inv1 = inv + mm3(split(wq), w_s, ((1,), (1,)))
    full_s = split(
        jnp.concatenate(
            [jnp.concatenate([inv1, -wq], axis=1), jnp.concatenate([-wq.T, inv2], axis=1)], axis=0
        )
    )

    for i in range(4):
        cols = slice(256 * i, 256 * i + 256)
        g = mm3(full_s, split(cpl[0:256, cols]))
        gv[:, cols] = g
        gh[:, cols], gl[:, cols] = split(g)

    def gain_copy(dx):
        xx = xs(dx)
        rows = pl.ds(pl.multiple_of(32 * z + 8 * xx, 8), 8)
        return remote(gv.at[rows], pgr.at[jq], gs_s.at[dx], gs_r.at[dx], dev(c, z, xx))

    @pl.when(own == c)
    def _():
        for dx in (2, 1, 3):
            gain_copy(dx).start()
        pgr[jq] = gv[pl.ds(pl.multiple_of(32 * z + 8 * x, 8), 8), :]

    for i in range(4):
        cols = slice(256 * i, 256 * i + 256)
        v = cpl[256:320, cols] - mm3(cpl_own, (gh[:, cols], gl[:, cols]))
        pcv[:, :, cols] = v.reshape(4, 16, 256)

    def cost_copy(dx):
        return remote(pcv.at[xs(dx)], pcr.at[jq, c], cs_s.at[dx], cs_r.at[dx, c], dev(own, z, xs(dx)))

    way = 1 - 2 * c
    source = xs(-way)

    def cost_near():
        return remote(pcv.at[xs(2)], cost_via, via_s.at[0], via_r.at[0], dev(c, z, xs(way)))

    def cost_onward():
        return remote(
            cost_via, pcr.at[lax.rem(source, 2), c], on_s.at[0], cs_r.at[2, c], dev(source // 2, z, xs(way))
        )

    cost_near().start()
    for dx in (1, 3):
        cost_copy(dx).start()

    @pl.when(own == c)
    def _():
        pcr[jq, c] = pcv[x]

    @pl.when(own != c)
    def _():
        cost_copy(0).start()

    for d in range(2):
        cov_onward(d, True).wait_recv()
        cov_far_hand(d, c).start()

    a_rows = a5[z, :, c].reshape(64, 1024).astype(F32)
    b_rows = b5[z, :, c].reshape(64, 256)
    closed = (a_rows - (mm(b_rows, gh[...]) + mm(b_rows, gl[...]))).astype(BF16)
    cl2[:, 0:1024] = closed
    cl2[:, 1024:1536] = closed[:, 0:512]
    for dz in (0,) + NEAR:
        cov_hand(dz, oc).wait_recv()
    for d in range(2):
        cov_far_hand(d, oc).wait_recv()
    nt = ((1,), (1,))
    for q in range(8):
        low = (q - BLOCKS + 1) % 8
        right = jnp.concatenate(
            [
                p5[(low + i) % 8, :, :, :, 128 * (BLOCKS - 1 - i) : 128 * (BLOCKS - i)].reshape(128, 128)
                for i in range(BLOCKS)
            ],
            axis=0,
        )
        mom[:, 128 * q : 128 * q + 128] = mm(cl2[:, 128 * low : 128 * (low + BLOCKS)], right) + mm(
            cl2[:, 128 * (q + 1) : 128 * (q + 4)], p5[q, :, :, :, 128:512].reshape(128, 384), nt
        )
    moment_s = split(mom[...])
    inner_s = split(mm3(moment_s, (gh[...], gl[...]), nt))

    cost_near().wait_recv()
    cost_onward().start()

    def spread_copy(dx, half):
        cols = pl.ds(512 * half, 512)
        return remote(
            spv.at[xs(dx), :, cols], spr.at[x, c, :, cols], ss_s.at[dx, half], ss_r.at[dx, half], dev(c, z, xs(dx))
        )

    def spread_got(dx, half):
        cols = pl.ds(512 * half, 512)
        return remote(
            spv.at[xs(dx), :, cols], spr.at[xs(-dx), c, :, cols], ss_s.at[dx, half], ss_r.at[dx, half], dev(c, z, xs(dx))
        )

    def spread_hand(dx, half, core):
        part = spr.at[xs(-dx), core, :, pl.ds(512 * half, 512)]
        return remote(part, part, sf_s.at[dx, half], sf_r.at[dx, half], pair)

    def spread_near(half):
        return remote(
            spv.at[xs(2), :, pl.ds(512 * half, 512)], spread_via.at[half],
            via_s.at[1 + half], via_r.at[1 + half], dev(c, z, xs(way)),
        )

    def spread_onward(half):
        return remote(
            spread_via.at[half], spr.at[source, c, :, pl.ds(512 * half, 512)],
            on_s.at[1 + half], ss_r.at[2, half], dev(c, z, xs(way)),
        )

    for half in range(2):
        for i in range(2):
            cols = slice(512 * half + 256 * i, 512 * half + 256 * i + 256)
            v = mm2(moment_s, at5[:, :, :, :, cols].reshape(1024, 256)) - mm2(inner_s, lt[0:256, cols])
            spv[:, :, cols] = v.reshape(4, 16, 256)

        spread_near(half).start()
        cols = slice(512 * half, 512 * half + 512)
        spr[x, c, :, cols] = spv[x, :, cols]
        spread_hand(0, half, c).start()

    for half in range(2):
        for dx in (1, 3):
            spread_copy(dx, half).start()
    for half in range(2):
        spread_near(half).wait_recv()
        spread_onward(half).start()

    for cp in swap + spread_e:
        cp.wait_send()
    for dx in range(4):
        @pl.when(xs(dx) // 2 == c)
        def _(dx=dx):
            cov_copy(dx, True).wait_send()
            if dx:
                cov_copy(dx, False).wait_send()
    drain(*e_ring)
    cov_hand(0, c).wait_send()
    for dz in NEAR:
        cov_send(dz).wait_send()
        cov_hand(dz, c).wait_send()
    for d in range(2):
        cov_onward(d).wait_send()
        cov_far_hand(d, c).wait_send()

    for dx in (1, 2, 3):
        @pl.when(xs(-dx) // 2 == c)
        def _(dx=dx):
            remote(gv.at[0:8], pgr.at[lax.rem(xs(-dx), 2)], gs_s.at[dx], gs_r.at[dx], pair).wait_recv()
            for core in range(2):
                remote(pcv.at[0], pcr.at[lax.rem(xs(-dx), 2), core], cs_s.at[dx], cs_r.at[dx, core], pair).wait_recv()

    @pl.when(own == c)
    def _():
        remote(pcv.at[0], pcr.at[jq, oc], cs_s.at[0], cs_r.at[0, oc], pair).wait_recv()

    out_pg = pltpu.make_async_copy(pgr, pgr_out, out_sem.at[0])
    out_pg.start()
    out_pc = pltpu.make_async_copy(pcr, pcr_out, out_sem.at[1])
    out_pc.start()

    for half in range(2):
        for dx in (1, 3, 2):
            spread_got(dx, half).wait_recv()
            spread_hand(dx, half, c).start()
    out_own = pltpu.make_async_copy(spr.at[:, c], spr_out.at[:, c], out_sem.at[2])
    out_own.start()
    for half in range(2):
        for dx in range(4):
            spread_hand(dx, half, oc).wait_recv()
    out_pair = pltpu.make_async_copy(spr.at[:, oc], spr_out.at[:, oc], out_sem.at[3])
    out_pair.start()

    @pl.when(own == c)
    def _():
        for dx in (2, 1, 3):
            gain_copy(dx).wait_send()

    @pl.when(own != c)
    def _():
        cost_copy(0).wait_send()

    cost_near().wait_send()
    cost_onward().wait_send()
    for half in range(2):
        spread_near(half).wait_send()
        spread_onward(half).wait_send()
    for dx in (1, 3):
        cost_copy(dx).wait_send()
        for half in range(2):
            spread_copy(dx, half).wait_send()
    for half in range(2):
        for dx in range(4):
            spread_hand(dx, half, c).wait_send()
    out_pg.wait()
    out_pc.wait()
    out_own.wait()
    out_pair.wait()


def finish(po, sw, nz, pcr, pgr, spr, pc_out, pg_out, ch_out, pc, pg, ch, out_sem):
    outs = [
        pltpu.make_async_copy(pg, pg_out, out_sem.at[8]),
        pltpu.make_async_copy(pc, pc_out, out_sem.at[9]),
    ]
    c, y, z, x = place()
    zlane = pl.ds(pl.multiple_of(z * 128, 128), 128)
    diag = lax.broadcasted_iota(jnp.int32, (32, 128), 1) == (
        32 * x + lax.broadcasted_iota(jnp.int32, (32, 128), 0)
    )
    pick = lax.broadcasted_iota(jnp.int32, (32, 32), 1) == lax.broadcasted_iota(jnp.int32, (32, 32), 0)

    def on_diag(row):
        column = jnp.sum(jnp.where(pick, row, 0.0), axis=1, keepdims=True)
        return jnp.where(diag, column, 0.0).reshape(2, 16, 128)

    for k in range(8):
        parent = [po[k] == 4 * y + q for q in range(4)]

        def fill(i, _):
            cols = pl.ds(pl.multiple_of(i * 256, 256), 256)
            v = spr[0, :, :, cols]
            for q in range(1, 4):
                v = jnp.where(parent[q], spr[q, :, :, cols], v)
            ch[k, :, :, cols] = v
            return 0

        lax.fori_loop(0, 4, fill, 0)
        ch[k, :, :, zlane] += on_diag(nz[k : k + 1, :])
        outs.append(pltpu.make_async_copy(ch.at[k], ch_out.at[k], out_sem.at[k]))
        outs[-1].start()
        if k == 1:
            pg[...] = pgr[...]
            outs[0].start()
            pc[...] = pcr[...]
            for j in range(2):
                pc[j, :, :, zlane] += on_diag(sw[j : j + 1, :])
            outs[1].start()
    for cp in outs:
        cp.wait()


def on_device(cc, cw, po, a, b, sw, iw, pcov, nz):
    any_, vmem, smem = (pl.BlockSpec(memory_space=m) for m in (pl.ANY, pltpu.VMEM, pltpu.SMEM))
    v, dma = pltpu.VMEM, pltpu.SemaphoreType.DMA
    scratch = [
        v((8, 32, 1024), F32),
        v((8, 4, 2, 16, 1024), BF16),
        v((8, 4, 2, 16, 256), BF16),
        v((8, 4, 2, 16, 1024), BF16),
        v((320, 1536), BF16),
        v((8, 4, 2, 16, 128 * BLOCKS + 128), BF16),
        v((8, 4, 2, 16, 128 * BLOCKS), BF16),
        v((320, 1024), F32),
        v((4, 2, 16, 1024), F32),
        v((4, 16, 1024), F32),
        v((8, 128), F32),
        v((8, 128), F32),
        v((2, 256), F32),
        v((2, 256), F32),
        v((2, 32, 1024), BF16),
        v((2, 32, 128 * BLOCKS), BF16),
        v((4, 16, 128 * BLOCKS + 128), BF16),
        v((320, 1024), BF16),
        v((320, 1024), BF16),
        v((320, 1024), F32),
        v((256, 1024), F32),
        v((256, 1024), BF16),
        v((256, 1024), BF16),
        v((64, 1536), BF16),
        v((64, 1024), F32),
        v((4, 16, 1024), F32),
        v((2, 2, 16, 1024), F32),
        v((2, 8, 1024), F32),
        v((4, 16, 1024), F32),
        v((4, 2, 16, 1024), F32),
        v((16, 1024), F32),
        v((2, 16, 512), F32),
        pltpu.SMEM((8,), jnp.int32), pltpu.SMEM((8,), jnp.int32),
        dma((7,)), dma((1,)), dma((4,)),
        dma((3,)), dma((3,)),
        dma((4,)), dma((4,)),
        dma((4, 2)), dma((4,)),
        dma((2, 4, 4)), dma((2, 4, 4)), dma((2, 5, 4)), dma((2, 5, 4)),
        dma((7,)), dma((7,)), dma((7,)), dma((7,)), dma((4,)), dma((4,)),
        dma((4,)), dma((4,)),
        dma((4,)), dma((4, 2)),
        dma((4, 2)), dma((4, 2)), dma((4, 2)), dma((4, 2)),
        dma((3,)), dma((3,)), dma((3,)),
    ]
    pcr, pgr, spr = pl.pallas_call(
        kernel,
        out_shape=(v((2, 2, 16, 1024), F32), v((2, 8, 1024), F32), v((4, 2, 16, 1024), F32)),
        in_specs=[any_] * 7,
        out_specs=(any_, any_, any_),
        scratch_shapes=scratch,
        compiler_params=pltpu.CompilerParams(collective_id=0, has_side_effects=True),
    )(cw, po, cc, a.reshape(8, 4, 2, 16, 1024), b.reshape(8, 4, 2, 16, 256), iw, pcov)
    pc, pg, ch = pl.pallas_call(
        finish,
        out_shape=(
            jax.ShapeDtypeStruct((2, 2, 16, 1024), F32),
            jax.ShapeDtypeStruct((2, 8, 1024), F32),
            jax.ShapeDtypeStruct((8, 2, 16, 1024), F32),
        ),
        in_specs=[smem] + [vmem] * 5,
        out_specs=(any_, any_, any_),
        scratch_shapes=[
            v((2, 2, 16, 1024), F32), v((2, 8, 1024), F32), v((8, 2, 16, 1024), F32), dma((10,)),
        ],
        compiler_params=pltpu.CompilerParams(vmem_limit_bytes=8 * 2**20),
    )(po, sw, nz, pcr, pgr, spr)
    return pc.reshape(2, 32, 1024), pg, ch.reshape(8, 32, 1024)


def solution(mesh):
    rows = P("node", "tile", None)
    placed = (rows, P("node"), P("node"), P(), P(), P("node", "tile"), P("node", None), rows, P("node", "tile"))
    return jax.shard_map(
        on_device, mesh=mesh, in_specs=placed, out_specs=(rows, rows, rows), check_vma=False
    )
```
